128 devices in a mesh: dp: 32 (over z, y, core), tensor: 4 (over x).
Axes of the slice: x: 4, y: 4, z: 4, core: 2. Of those that a mesh axis runs over, the one named last changes fastest.
Arguments:
- block_input: bfloat16 [12288, 2560], P('dp', 'tensor'), may hold values from -6 to 6
- gate_act: bfloat16 [12288, 6912], P('dp', 'tensor'), may hold values from -8 to 8
- grad_out: bfloat16 [12288, 2560], P('dp', 'tensor'), may hold values from -8 to 8
- up_weight: bfloat16 [2560, 6912], P('dp', 'tensor'), may hold values from -0.125 to 0.125
- down_weight: bfloat16 [6912, 2560], P('tensor', 'dp'), may hold values from -0.078125 to 0.078125
- quant_step: float32 [6912], P('tensor'), as said below
- round_logit: float32 [2560, 6912], P('dp', 'tensor'), may hold values from -48 to 48
- grid_offset: bfloat16 [2560, 6912], P('dp', 'tensor'), may hold values from 0 to 1
Outputs:
- block_output: bfloat16 [12288, 2560], P('dp', 'tensor')
- fisher: bfloat16 [12288, 6912], P('dp', 'tensor')
- grad_logit: float32 [2560, 6912], P('dp', 'tensor')
- loss: float32 [], replicated
The draws below stay inside these ranges and needn't reach their ends.
Inputs may be any that keep to these rules, and one draw needn't show every extreme that they name: `quant_step`: positive steps between 0.8 and 3.2 divided by the square root of 2560.
All inputs are finite; a program needn't handle non-finite values.
Results may differ from the reference program's by a relative error of at most 0.022.
Values may be sent and summed in bfloat16 or wider, within the bound.
A program may use at most 128 MiB of HBM per device.

```python
import jax
import jax.numpy as jnp
from jax import lax

D = 2560
FFW = 6912
TOK_DEV = 384
TOKENS = 12288
N_DP = 32
N_TENSOR = 4


def draw_grad_out(key, part):
    key_noise, key_rows = jax.random.split(jax.random.fold_in(key, 11), 2)
    position = jnp.arange(TOKENS, dtype=jnp.float32) / max(TOKENS - 1, 1)
    jitter = jax.random.uniform(key_rows, (TOKENS,), jnp.float32)
    noise = jnp.clip(jax.random.normal(key_noise, (TOKENS, D), jnp.float32), -4.0, 4.0)
    row_scale = 0.3 * jnp.sqrt(10.0 ** (0.5 * position + 0.5 * jitter))
    values = row_scale[:, None] * noise
    return values.astype(jnp.bfloat16)


def draw_gate_act(key, part):
    key_noise, key_cols = jax.random.split(jax.random.fold_in(key, 23), 2)
    position = jnp.arange(FFW, dtype=jnp.float32) / max(FFW - 1, 1)
    jitter = jax.random.uniform(key_cols, (FFW,), jnp.float32)
    noise = jnp.clip(jax.random.normal(key_noise, (TOKENS, FFW), jnp.float32), -4.0, 4.0)
    col_scale = 0.5 * jnp.sqrt(10.0 ** (0.5 * position + 0.5 * jitter))
    values = col_scale[None, :] * noise
    return values.astype(jnp.bfloat16)


def draw_quant_step(key, part):
    key_steps = jax.random.fold_in(key, 53)
    factor = jnp.exp(jax.random.uniform(key_steps, (FFW,), jnp.float32, jnp.log(0.8), jnp.log(3.2)))
    return factor * (1.0 / jnp.sqrt(jnp.float32(D)))


def draw_round_logit(key, part):
    key_noise, key_rows = jax.random.split(jax.random.fold_in(key, 37), 2)
    position = jnp.arange(D, dtype=jnp.float32) / max(D - 1, 1)
    jitter = jax.random.uniform(key_rows, (D,), jnp.float32, 0.8, 1.2)
    noise = jax.random.uniform(key_noise, (D, FFW), jnp.float32, -1.0, 1.0)
    amplitude = 30.0 * (0.2 / 30.0) ** position * jitter
    values = amplitude[:, None] * noise
    return values


def with_spikes(entries, own_key, source, target, parts, factor):
    owner, partner = [(jnp.arange(entries.shape[axis_at]) // (entries.shape[axis_at] // parts)).reshape([-1 if axis == axis_at else 1 for axis in range(entries.ndim)]) for axis_at in (source, target)]
    chosen = jax.random.permutation(own_key, parts)[partner]
    strong = (owner == chosen) | (owner == (partner + parts // 2) % parts)
    return jnp.where(strong, factor * entries, entries)


def shard_levels(key, extent, pieces, smallest, top_value):
    factor_of, own = 1.0, jax.random.fold_in(key, 6)
    for axis_at, shards_of in pieces:
        steps = jnp.exp(jax.random.uniform(jax.random.fold_in(own, axis_at), (shards_of,), jnp.float32, smallest / len(pieces), top_value / len(pieces)))
        factor_of = factor_of * jnp.repeat(steps, extent[axis_at] // shards_of).reshape([-1 if axis == axis_at else 1 for axis in range(len(extent))])
    return factor_of


def normal_values(stream_key, shape, spread, most, shards=(), held_as=jnp.bfloat16):
    drawn = spread * jax.random.normal(stream_key, shape, jnp.float32)
    if shards:
        drawn = drawn * shard_levels(stream_key, shape, shards, -0.22, 0.18)
    return jnp.clip(drawn, -most, most).astype(held_as)


def gaussian_with(rng, dims, deviation, reach, shards, heavy, kind=jnp.bfloat16):
    result = deviation * jax.random.normal(rng, dims, jnp.float32)
    if shards:
        result = result * shard_levels(rng, dims, shards, -0.22, 0.18)
    return jnp.clip(with_spikes(result, jax.random.fold_in(rng, 3), *heavy), -reach, reach).astype(kind)


def setup_inputs(seed: int = 0) -> dict:
    seeds = jax.random.split(jax.random.key(seed), 9)
    return {
        "block_input": gaussian_with(seeds[0], (TOKENS, D), 1.0, 6.0, ((0, 32), (1, 4)), (0, 1, 32, 2.75)),
        "gate_act": draw_gate_act(jax.random.fold_in(seeds[8], 71), 0),
        "grad_out": draw_grad_out(jax.random.fold_in(seeds[8], 71), 0),
        "up_weight": normal_values(seeds[3], (D, FFW), D ** -0.5, 0.125, ((0, 32), (1, 4))),
        "down_weight": normal_values(seeds[4], (FFW, D), FFW ** -0.5, 0.078125, ((0, 4), (1, 32))),
        "quant_step": draw_quant_step(jax.random.fold_in(seeds[8], 71), 0),
        "round_logit": draw_round_logit(jax.random.fold_in(seeds[8], 71), 0),
        "grid_offset": jnp.clip(1.0 * jax.random.uniform(seeds[7], (D, FFW), jnp.float32) ** shard_levels(seeds[7], (D, FFW), ((0, 32), (1, 4)), -0.2, 0.2), 0.0, 1.0).astype(jnp.bfloat16),
    }


reg_weight = 0.5


def rounded(values):
    low = lax.optimization_barrier(values.astype(jnp.bfloat16))
    return low.astype(jnp.float32)


def reference(block_input, gate_act, grad_out, up_weight, down_weight, quant_step, round_logit, grid_offset):
    up_proj = jnp.dot(block_input, up_weight, preferred_element_type=jnp.float32)
    hidden = (gate_act.astype(jnp.float32) * up_proj).astype(jnp.bfloat16)
    group_size = FFW // N_TENSOR
    out_total = jnp.zeros((TOKENS, D), jnp.float32)
    for group in range(N_TENSOR):
        lower = group * group_size
        partial_out = jnp.dot(hidden[:, lower:lower + group_size], down_weight[lower:lower + group_size, :], preferred_element_type=jnp.float32)
        out_total = out_total + rounded(partial_out)
    block_output = out_total.astype(jnp.bfloat16)
    grad_hidden = lax.dot_general(grad_out, down_weight, (((1,), (1,)), ((), ())), preferred_element_type=jnp.float32)
    fisher = ((grad_hidden * gate_act.astype(jnp.float32)) ** 2).astype(jnp.bfloat16)
    fisher_vals = fisher.astype(jnp.float32)
    soft_bits = jax.nn.sigmoid(round_logit)
    weight_delta = (quant_step[None, :] * (soft_bits - grid_offset.astype(jnp.float32))).astype(jnp.bfloat16)
    residual = jnp.dot(block_input, weight_delta, preferred_element_type=jnp.float32)
    weighted = (fisher_vals * residual).astype(jnp.bfloat16)
    input_groups = block_input.reshape(N_DP, TOK_DEV, D)
    weighted_groups = weighted.reshape(N_DP, TOK_DEV, FFW)

    def add_group(running, operands):
        rows_in, rows_weighted = operands
        product = lax.dot_general(rows_in, rows_weighted, (((0,), (0,)), ((), ())), preferred_element_type=jnp.float32)
        return running + rounded(product), None

    grad_sum, unused = lax.scan(add_group, jnp.zeros((D, FFW), jnp.float32), (input_groups, weighted_groups))
    total_cells = TOKENS * FFW
    weight_cells = D * FFW
    fisher_mean = jnp.sum(fisher_vals) / total_cells
    centered = 2.0 * soft_bits - 1.0
    sig_slope = soft_bits * (1.0 - soft_bits)
    grad_logit = grad_sum * (2.0 / fisher_mean) * quant_step[None, :] * sig_slope - reg_weight * 8.0 * centered ** 3 * sig_slope
    recon_total = jnp.sum(fisher_vals * residual * residual)
    reg_total = jnp.sum(1.0 - (centered * centered) ** 2)
    loss = recon_total / (fisher_mean * total_cells) + reg_weight * reg_total / weight_cells
    return block_output, fisher, grad_logit, loss
```

```python
import jax
import jax.numpy as jnp
from jax import lax
from jax.experimental import pallas as pl
from jax.experimental.pallas import tpu as pltpu
from jax.sharding import Mesh
from jax.sharding import PartitionSpec as P

D = 2560
FFW = 6912
TOK = 384
FF = 1728
FFP = 1792
ROWS = 80
XW = 640
TILE = 256
NT = FFP // TILE
REG_WEIGHT = 0.5
BF = jnp.bfloat16
F32 = jnp.float32
MESH = pl.DeviceIdType.MESH

GATHER = (("y", "z", 1), ("z", "y", 1), ("y", "z", -1), ("z", "y", -1))
REDUCE = (("z", "y", 1), ("y", "z", 1), ("z", "y", -1), ("y", "z", -1))
COLS = ((0, 512), (512, 512), (1024, 384), (1408, 384))
GATHER_COLS = ((0, 1, 2, 3), (2, 3, 0, 1), (0, 1, 2, 3))
REDUCE_COLS = (2, 3, 0, 1)
SUBS = 3
SUB_ROWS = TOK // 2 // SUBS


def kernel(
    w_in, bi, go, gate_in, reg_in,
    block_out, fisher_out, gsum, stats,
    full, xf, feats_t, gate, fish, wbuf, grad, pair, ring, outp, outr, reg, acc, stat,
    local, ag_recv, ag_send, pr_recv, pr_send, x_recv, x_send,
    rs_recv, rs_send, pe_recv, pe_send, xo_recv, xo_send, st_recv, st_send,
):
    me = {name: lax.axis_index(name) for name in ("z", "y", "c", "x")}
    z, y, c, x = me["z"], me["y"], me["c"], me["x"]
    other = {"c": 1 - c}

    def at(axis, k):
        return lax.rem(me[axis] + (k + 4), 4)

    def step_to(axis, sign):
        return {axis: at(axis, sign)}

    def remote(src, dst, send, recv, device):
        return pltpu.make_async_remote_copy(
            src_ref=src, dst_ref=dst, send_sem=send, recv_sem=recv, device_id=device, device_id_type=MESH
        )

    def back(axis, sign, k):
        return lax.rem(me[axis] + (4 - k if sign > 0 else k), 4)

    def ahead(axis, sign, k):
        return lax.rem(me[axis] + (k if sign > 0 else 4 - k), 4)

    def cols_of(a, s):
        lo, width = COLS[GATHER_COLS[a][s]]
        return pl.ds(lo, width)

    def piece(a, s, d, e):
        first, second, sign = GATHER[s]
        co = {first: back(first, sign, d), second: back(second, sign, e)}
        return full.at[a, co["z"], co["y"], c, :, cols_of(a, s)]

    def send_first(a, s, d):
        first, second, sign = GATHER[s]
        ref = piece(a, s, d, 0)
        remote(ref, ref, ag_send.at[a, s], ag_recv.at[a, s, d + 1], step_to(first, sign)).start()

    def send_second(a, s, d, e):
        first, second, sign = GATHER[s]
        ref = piece(a, s, d, e)
        remote(ref, ref, ag_send.at[a, s], ag_recv.at[a, s, (e + 1) * 4 + d], step_to(second, sign)).start()

    def wait_piece(a, s, d, e):
        ref = piece(a, s, d, e)
        remote(ref, ref, ag_send.at[a, s], ag_recv.at[a, s, e * 4 + d], other).wait_recv()

    def bundle(a, s, e, parity):
        first, second, sign = GATHER[s]
        g = back(second, sign, e)
        if second == "z":
            return full.at[a, g, :, parity, :, cols_of(a, s)]
        return full.at[a, :, g, parity, :, cols_of(a, s)]

    def send_pair(a, s, e):
        ref = bundle(a, s, e, c)
        remote(ref, ref, pr_send.at[a, s], pr_recv.at[a, s, e], other).start()

    def ag_start(a):
        for s in range(4):
            send_first(a, s, 0)
            send_second(a, s, 0, 0)

    def ag_first(a, d):
        for s in range(4):
            wait_piece(a, s, d, 0)
            if d < 3:
                send_first(a, s, d)
            send_second(a, s, d, 0)
            if d == 3:
                send_pair(a, s, 0)

    def ag_second(a, k):
        e, d = 1 + k // 4, lax.rem(k, 4)
        for s in range(4):
            wait_piece(a, s, d, e)

            @pl.when(e < 3)
            def _():
                send_second(a, s, d, e)

            @pl.when(d == 3)
            def _():
                send_pair(a, s, e)

    def ag_finish(a):
        for s in range(4):
            for e in range(4):
                ref = bundle(a, s, e, 1 - c)
                remote(ref, ref, pr_send.at[a, s], pr_recv.at[a, s, e], other).wait_recv()

    def ag_drain(a):
        for s in range(4):
            ref = ring.at[:, :, cols_of(a, s)]
            remote(ref, ref, ag_send.at[a, s], ag_recv.at[a, s, 0], other).wait_send()
            ref = full.at[a, :, :, c, :, cols_of(a, s)]
            remote(ref, ref, pr_send.at[a, s], pr_recv.at[a, s, 0], other).wait_send()

    def x_block(t, k, lo, count):
        return xf.at[t, pl.ds(lo, count), pl.ds(pl.multiple_of(at("x", k) * XW, XW), XW)]

    X_MOVES = ((0, 1, 0, TOK, -1), (0, -1, 0, TOK, 1), (-1, 1, 0, TOK // 2, 2), (1, -1, TOK // 2, TOK // 2, 2))

    def x_copy(t, i, k):
        src, sign, lo, count, got = X_MOVES[i]
        ref = x_block(t, k, lo, count)
        return remote(ref, ref, x_send.at[t, i], x_recv.at[t, i], step_to("x", sign))

    def x_start(t, i):
        x_copy(t, i, X_MOVES[i][0]).start()

    def x_wait(t, i):
        x_copy(t, i, X_MOVES[i][4]).wait_recv()

    def r_cols(s):
        lo, width = COLS[REDUCE_COLS[s]]
        return pl.ds(lo, width)

    def pair_copy(s):
        return remote(
            grad.at[:, :, 1 - c, :, r_cols(s)], pair.at[:, :, :, r_cols(s)], pe_send.at[s], pe_recv.at[s], other
        )

    def ring_copy(s, src, slot, device):
        return remote(src, ring.at[slot, :, r_cols(s)], rs_send.at[s], rs_recv.at[s, slot], device)

    def rs_step(s, t, j):
        first, second, sign = REDUCE[s]
        cols = r_cols(s)
        co = {first: ahead(first, sign, 3 - t), second: ahead(second, sign, 3 - j)}
        mine = grad.at[co["z"], co["y"], c, :, cols]
        total = mine[...].astype(F32) + pair[co["z"], co["y"], :, cols].astype(F32)

        def arrived(slot):
            ring_copy(s, mine, slot, other).wait_recv()
            return ring[slot, :, cols].astype(F32)

        if t > 0:
            total = total + arrived((t - 1) * 4 + j)
        if t < 3:
            mine[...] = total.astype(BF)
            ring_copy(s, mine, t * 4 + j, step_to(first, sign)).start()
            return
        if j > 0:
            total = total + arrived(12 + j - 1)
        if j < 3:
            mine[...] = total.astype(BF)
            ring_copy(s, mine, 12 + j, step_to(second, sign)).start()
        else:
            gsum[:, cols] = total

    def xo_rows(way, sub):
        return pl.ds(way * (TOK // 2) + sub * SUB_ROWS, SUB_ROWS)

    def xo_copy(way, sub, t):
        sign = 1 - 2 * way
        rows = xo_rows(way, sub)
        return remote(
            outp.at[ahead("x", sign, 3 - t), rows, :], outr.at[t, rows, :],
            xo_send.at[way, sub, t], xo_recv.at[way, sub, t], step_to("x", sign),
        )

    def xo_step(way, sub, t):
        sign = 1 - 2 * way
        rows = xo_rows(way, sub)
        if t > 0:
            own = ahead("x", sign, 3 - t)
            xo_copy(way, sub, t - 1).wait_recv()
            total = outp[own, rows, :].astype(F32) + outr[t - 1, rows, :].astype(F32)
            if t == 3:
                block_out[rows, :] = total.astype(BF)
                return
            outp[own, rows, :] = total.astype(BF)
        xo_copy(way, sub, t).start()

    ST_AXES = (("y", 4), ("z", 4), ("x", 4), ("c", 2))

    def st_copy(ph, slot, k):
        axis, size = ST_AXES[ph]
        device = {axis: lax.rem(me[axis] + k, size)}
        ref = stat.at[ph, slot]
        return remote(ref, ref, st_send.at[ph, k], st_recv.at[ph, slot], device)

    def st_start(ph, total):
        axis, size = ST_AXES[ph]
        stat[ph, me[axis]] = total
        for k in range(1, size):
            st_copy(ph, me[axis], k).start()

    def st_finish(ph):
        axis, size = ST_AXES[ph]
        for k in range(1, size):
            st_copy(ph, lax.rem(me[axis] + k, size), k).wait_recv()
        total = stat[ph, 0]
        for k in range(1, size):
            total = total + stat[ph, k]
        return total

    def tile(n):
        return pl.ds(pl.multiple_of(n * TILE, TILE), TILE)

    def weights(a, n):
        return full[a, :, :, :, :, tile(n)].reshape(D, TILE)

    def fold(v):
        v = jnp.sum(v.reshape(TOK // 8, 8, TILE), axis=0)
        return v[:, :128] + v[:, 128:]

    def fisher_tile(n):
        product = jnp.dot(xf[0], weights(0, n), preferred_element_type=F32)
        value = ((product * gate[:, tile(n)].astype(F32)) ** 2).astype(BF)
        fish[:, tile(n)] = value
        acc[0] += fold(value.astype(F32))

    def residual_tile(n):
        residual = jnp.dot(xf[1], weights(1, n), preferred_element_type=F32)
        weighted = fish[:, tile(n)].astype(F32) * residual
        wbuf[:, tile(n)] = weighted.astype(BF)
        acc[1] += fold(weighted * residual)

    def grad_tile(n):
        right = wbuf[:, tile(n)]
        for part in range(4):
            product = jnp.dot(feats_t[part], right, preferred_element_type=F32)
            grad[part, :, :, :, tile(n)] = product.astype(BF).reshape(4, 2, ROWS, TILE)

    def hidden_tile(n):
        product = jnp.dot(xf[1], weights(2, n), preferred_element_type=F32)
        wbuf[:, tile(n)] = (product * gate[:, tile(n)].astype(F32)).astype(BF)

    def out_tile(i):
        target = at("x", 3 - 2 * i + (i // 2) * 3)
        right = full[0, target].reshape(XW, FFP)
        product = lax.dot_general(wbuf[...], right, (((1,), (1,)), ((), ())), preferred_element_type=F32)
        outp[target] = product.astype(BF)

    own_cols = pl.ds(pl.multiple_of(x * XW, XW), XW)
    loads = [pltpu.make_async_copy(w_in.at[a], full.at[a, z, y, c], local.at[a]) for a in range(3)]
    loads += [
        pltpu.make_async_copy(go, xf.at[0, :, own_cols], local.at[3]),
        pltpu.make_async_copy(bi, xf.at[1, :, own_cols], local.at[4]),
        pltpu.make_async_copy(gate_in, gate, local.at[5]),
        pltpu.make_async_copy(reg_in, reg, local.at[6]),
    ]
    for load in loads:
        load.start()
    barrier = pltpu.get_barrier_semaphore()
    partners = [{axis: at(axis, k)} for axis in ("z", "y", "x") for k in (1, 2, 3)] + [other]
    for device in partners:
        pl.semaphore_signal(barrier, inc=1, device_id=device, device_id_type=MESH)
    acc[...] = jnp.zeros_like(acc)
    pl.semaphore_wait(barrier, len(partners))
    for load in loads:
        load.wait()

    for i in (0, 1):
        x_start(0, i)
    ag_start(0)
    for i in (0, 1):
        x_start(1, i)
    ag_start(1)
    for d in (1, 2, 3):
        ag_first(0, d)
    for i in (0, 1):
        x_wait(0, i)
    for i in (2, 3):
        x_start(0, i)

    @pl.loop(0, 12)
    def _(k):
        ag_second(0, k)

    ag_start(2)
    for d in (1, 2, 3):
        ag_first(1, d)
    for i in (2, 3):
        x_wait(0, i)
    for i in (0, 1):
        x_wait(1, i)
    for i in (2, 3):
        x_start(1, i)
    ag_finish(0)

    @pl.loop(0, NT)
    def _(n):
        @pl.when(n < 6)
        def _():
            ag_second(1, 2 * n)
            ag_second(1, 2 * n + 1)

        fisher_tile(n)

    save_fisher = pltpu.make_async_copy(fish, fisher_out, local.at[7])
    save_fisher.start()
    for i in (2, 3):
        x_wait(1, i)
    for part in range(4):
        feats_t[part] = jnp.transpose(xf[1, :, part * XW:(part + 1) * XW])
        if part < 3:
            ag_first(2, part + 1)
    ag_finish(1)

    @pl.loop(0, NT)
    def _(n):
        @pl.when(n < 6)
        def _():
            ag_second(2, 2 * n)
            ag_second(2, 2 * n + 1)

        residual_tile(n)
        grad_tile(n)
        for s in range(4):
            lo, width = COLS[REDUCE_COLS[s]]

            @pl.when(n == (lo + width - 1) // TILE)
            def _():
                pair_copy(s).start()

    acc[2] = reg[...]
    st_start(0, acc[...])
    by_ready = sorted(range(4), key=lambda s: REDUCE_COLS[s])
    for s in by_ready:
        pair_copy(s).wait_recv()

        @pl.loop(0, 4)
        def _(j):
            rs_step(s, 0, j)

    st_start(1, st_finish(0))
    ag_finish(2)

    @pl.loop(0, NT)
    def _(n):
        hidden_tile(n)

        @pl.when(n < 4)
        def _():
            for s in range(4):
                rs_step(s, 1, n)

        @pl.when(n >= 4)
        def _():
            for s in range(4):
                rs_step(s, 2, n - 4)

    for s in range(4):
        rs_step(s, 2, 3)
    st_start(2, st_finish(1))

    @pl.loop(0, 4)
    def _(i):
        out_tile(i)
        for way in range(2):
            @pl.when(i == way)
            def _():
                for sub in range(SUBS):
                    xo_step(way, sub, 0)

    st_start(3, st_finish(2))
    for t in (1, 2, 3):
        for s in range(4):
            rs_step(s, 3, t - 1)
        for sub in range(SUBS):
            for way in range(2):
                xo_step(way, sub, t)
    for s in range(4):
        rs_step(s, 3, 3)
    stats[...] = st_finish(3)

    for a in range(3):
        ag_drain(a)
    for t in range(2):
        for i in range(4):
            x_copy(t, i, X_MOVES[i][0]).wait_send()
    for s in range(4):
        pair_copy(s).wait_send()
        ref = ring.at[:, :, r_cols(s)]
        remote(ref, ref, rs_send.at[s], rs_recv.at[s, 0], other).wait_send()
    for way in range(2):
        for sub in range(SUBS):
            for t in range(3):
                xo_copy(way, sub, t).wait_send()
    for ph in range(4):
        for k in range(1, ST_AXES[ph][1]):
            st_copy(ph, me[ST_AXES[ph][0]], k).wait_send()
    save_fisher.wait()


def run(w_in, bi, go, gate_in, reg_in):
    vmem, hbm = pl.BlockSpec(memory_space=pltpu.VMEM), pl.BlockSpec(memory_space=pl.ANY)
    dma = pltpu.SemaphoreType.DMA
    return pl.pallas_call(
        kernel,
        out_shape=(
            jax.ShapeDtypeStruct((TOK, XW), BF),
            jax.ShapeDtypeStruct((TOK, FFP), BF),
            jax.ShapeDtypeStruct((ROWS, FFP), F32),
            jax.ShapeDtypeStruct((3, 8, 128), F32),
        ),
        in_specs=[hbm] * 5,
        out_specs=(vmem, hbm, vmem, vmem),
        scratch_shapes=[
            pltpu.VMEM((3, 4, 4, 2, ROWS, FFP), BF),
            pltpu.VMEM((2, TOK, D), BF),
            pltpu.VMEM((4, XW, TOK), BF),
            pltpu.VMEM((TOK, FFP), BF),
            pltpu.VMEM((TOK, FFP), BF),
            pltpu.VMEM((TOK, FFP), BF),
            pltpu.VMEM((4, 4, 2, ROWS, FFP), BF),
            pltpu.VMEM((4, 4, ROWS, FFP), BF),
            pltpu.VMEM((15, ROWS, FFP), BF),
            pltpu.VMEM((4, TOK, XW), BF),
            pltpu.VMEM((3, TOK, XW), BF),
            pltpu.VMEM((8, 128), F32),
            pltpu.VMEM((3, 8, 128), F32),
            pltpu.VMEM((4, 4, 3, 8, 128), F32),
            dma((8,)),
            dma((3, 4, 16)), dma((3, 4)), dma((3, 4, 4)), dma((3, 4)),
            dma((2, 4)), dma((2, 4)),
            dma((4, 16)), dma((4,)), dma((4,)), dma((4,)),
            dma((2, SUBS, 3)), dma((2, SUBS, 3)),
            dma((4, 4)), dma((4, 4)),
        ],
        compiler_params=pltpu.CompilerParams(
            collective_id=0, has_side_effects=True, vmem_limit_bytes=67043328
        ),
    )(w_in, bi, go, gate_in, reg_in)


def wide(a):
    return jnp.pad(a, ((0, 0), (0, FFP - FF)))


def body(
    block_input, gate_act, grad_out, up_weight, down_weight, quant_step, round_logit, grid_offset
):
    soft_bits = jax.nn.sigmoid(round_logit)
    weight_delta = (quant_step[None, :] * (soft_bits - grid_offset.astype(F32))).astype(BF)
    centered = 2.0 * soft_bits - 1.0
    reg_local = jnp.sum(1.0 - (centered * centered) ** 2)
    w_in = jnp.stack([wide(down_weight.T), wide(weight_delta), wide(up_weight)])
    reg_in = jnp.full((8, 128), reg_local * (1.0 / 1024.0), F32)
    block_output, fisher, grad_sum, stats = run(w_in, block_input, grad_out, wide(gate_act), reg_in)
    fisher_sum, recon_total, reg_total = (jnp.sum(stats[i]) for i in range(3))
    total_cells = 12288 * FFW
    weight_cells = D * FFW
    fisher_mean = fisher_sum / total_cells
    sig_slope = soft_bits * (1.0 - soft_bits)
    grad_logit = (
        grad_sum[:, :FF] * (2.0 / fisher_mean) * quant_step[None, :] * sig_slope
        - REG_WEIGHT * 8.0 * centered**3 * sig_slope
    )
    loss = recon_total / (fisher_mean * total_cells) + REG_WEIGHT * reg_total / weight_cells
    return (block_output, fisher[:, :FF], grad_logit, loss)


def solution(mesh):
    torus = Mesh(mesh.devices.reshape(4, 4, 2, 4), ("z", "y", "c", "x"))
    dp = ("z", "y", "c")
    in_specs = (
        P(dp, "x"), P(dp, "x"), P(dp, "x"), P(dp, "x"), P("x", dp), P("x"), P(dp, "x"), P(dp, "x"),
    )
    out_specs = (P(dp, "x"), P(dp, "x"), P(dp, "x"), P())
    return jax.shard_map(body, mesh=torus, in_specs=in_specs, out_specs=out_specs, check_vma=False)
```

```python
import jax
import jax.numpy as jnp
from jax import lax
from jax.experimental import pallas as pl
from jax.experimental.pallas import tpu as pltpu
from jax.sharding import Mesh
from jax.sharding import PartitionSpec as P

D = 2560
FFW = 6912
TOK = 384
FF = 1728
FFP = 1792
ROWS = 80
XW = 640
TILE = 256
NT = FFP // TILE
REG_WEIGHT = 0.5
CELLS = 12288 * FFW
WEIGHT_CELLS = D * FFW
BF = jnp.bfloat16
F32 = jnp.float32
MESH = pl.DeviceIdType.MESH

GATHER = (("y", "z", 1), ("z", "y", 1), ("y", "z", -1), ("z", "y", -1), ("z", "y", -1))
REDUCE = tuple((second, first, sign) for first, second, sign in GATHER)
PARTS = ((0, 48, 0, 768), (0, 48, 768, 768), (48, 32, 0, 1152), (0, 48, 1536, 256), (48, 32, 1152, 640))
STREAMS = len(PARTS)
READY = tuple((col + cols - 1) // TILE for _, _, col, cols in PARTS)
EARLY = tuple(s for s in range(STREAMS) if READY[s] < NT - 1)
LATE = tuple(s for s in range(STREAMS) if READY[s] == NT - 1)
SUBS = 3
SUB_ROWS = TOK // 2 // SUBS


def kernel(
    bi, gate_in, go, up_in, down_in, step_in, logit_in, offset_in,
    block_out, fisher_out, grad_logit, loss_out,
    full, xf, feats_t, gate, gate_t, fish, wbuf, grad, pair, ring, outp, outr, acc, stat,
    up_own, down_own, step_own, logit, offset, slope, pull, gsum,
    local, ag_recv, ag_send, pr_recv, pr_send, x_recv, x_send,
    rs_recv, rs_send, pe_recv, pe_send, xo_recv, xo_send, st_recv, st_send,
):
    me = {name: lax.axis_index(name) for name in ("z", "y", "c", "x")}
    z, y, c, x = me["z"], me["y"], me["c"], me["x"]
    other = {"c": 1 - c}

    def at(axis, k):
        return lax.rem(me[axis] + (k + 4), 4)

    def step_to(axis, sign):
        return {axis: at(axis, sign)}

    def remote(src, dst, send, recv, device):
        return pltpu.make_async_remote_copy(
            src_ref=src, dst_ref=dst, send_sem=send, recv_sem=recv, device_id=device, device_id_type=MESH
        )

    def back(axis, sign, k):
        return lax.rem(me[axis] + (4 - k if sign > 0 else k), 4)

    def ahead(axis, sign, k):
        return lax.rem(me[axis] + (k if sign > 0 else 4 - k), 4)

    def part(s):
        row, rows, col, cols = PARTS[s]
        return pl.ds(row, rows), pl.ds(col, cols)

    def piece(a, s, d, e):
        first, second, sign = GATHER[s]
        co = {first: back(first, sign, d), second: back(second, sign, e)}
        return full.at[a, co["z"], co["y"], c, *part(s)]

    def send_first(a, s, d):
        first, second, sign = GATHER[s]
        ref = piece(a, s, d, 0)
        remote(ref, ref, ag_send.at[a, s], ag_recv.at[a, s, d + 1], step_to(first, sign)).start()

    def send_second(a, s, d, e):
        first, second, sign = GATHER[s]
        ref = piece(a, s, d, e)
        remote(ref, ref, ag_send.at[a, s], ag_recv.at[a, s, (e + 1) * 4 + d], step_to(second, sign)).start()

    def wait_piece(a, s, d, e):
        ref = piece(a, s, d, e)
        remote(ref, ref, ag_send.at[a, s], ag_recv.at[a, s, e * 4 + d], other).wait_recv()

    def bundle(a, s, e, parity):
        first, second, sign = GATHER[s]
        g = back(second, sign, e)
        if second == "z":
            return full.at[a, g, :, parity, *part(s)]
        return full.at[a, :, g, parity, *part(s)]

    def send_pair(a, s, e):
        ref = bundle(a, s, e, c)
        remote(ref, ref, pr_send.at[a, s], pr_recv.at[a, s, e], other).start()

    def ag_start(a):
        for s in range(STREAMS):
            send_first(a, s, 0)
            send_second(a, s, 0, 0)

    def ag_first(a, d):
        for s in range(STREAMS):
            wait_piece(a, s, d, 0)

            @pl.when(d < 3)
            def _():
                send_first(a, s, d)

            send_second(a, s, d, 0)

            @pl.when(d == 3)
            def _():
                send_pair(a, s, 0)

    def ag_second(a, k):
        e, d = 1 + k // 4, k % 4
        for s in range(STREAMS):
            wait_piece(a, s, d, e)

            @pl.when(e < 3)
            def _():
                send_second(a, s, d, e)

            @pl.when(d == 3)
            def _():
                send_pair(a, s, e)

    def ag_finish(a):
        for s in range(STREAMS):
            for e in range(4):
                ref = bundle(a, s, e, 1 - c)
                remote(ref, ref, pr_send.at[a, s], pr_recv.at[a, s, e], other).wait_recv()

    def ag_drain(a):
        for s in range(STREAMS):
            ref = ring.at[:, *part(s)]
            remote(ref, ref, ag_send.at[a, s], ag_recv.at[a, s, 0], other).wait_send()
            ref = full.at[a, :, :, c, *part(s)]
            remote(ref, ref, pr_send.at[a, s], pr_recv.at[a, s, 0], other).wait_send()

    def x_block(t, k, lo, count):
        return xf.at[t, pl.ds(lo, count), pl.ds(pl.multiple_of(at("x", k) * XW, XW), XW)]

    X_MOVES = ((0, 1, 0, TOK, -1), (0, -1, 0, TOK, 1), (-1, 1, 0, TOK // 2, 2), (1, -1, TOK // 2, TOK // 2, 2))

    def x_copy(t, i, k):
        src, sign, lo, count, got = X_MOVES[i]
        ref = x_block(t, k, lo, count)
        return remote(ref, ref, x_send.at[t, i], x_recv.at[t, i], step_to("x", sign))

    def x_start(t, i):
        x_copy(t, i, X_MOVES[i][0]).start()

    def x_wait(t, i):
        x_copy(t, i, X_MOVES[i][4]).wait_recv()

    def pair_copy(s):
        return remote(
            grad.at[:, :, 1 - c, *part(s)], pair.at[:, :, *part(s)], pe_send.at[s], pe_recv.at[s], other
        )

    def ring_copy(s, src, slot, device):
        return remote(src, ring.at[slot, *part(s)], rs_send.at[s], rs_recv.at[s, slot], device)

    def rs_step(s, t, j):
        first, second, sign = REDUCE[s]
        co = {first: ahead(first, sign, 3 - t), second: ahead(second, sign, 3 - j)}
        mine = grad.at[co["z"], co["y"], c, *part(s)]
        total = mine[...].astype(F32) + pair[co["z"], co["y"], *part(s)].astype(F32)

        def arrived(slot):
            ring_copy(s, mine, slot, other).wait_recv()
            return ring[slot, *part(s)].astype(F32)

        if t > 0:
            total = total + arrived((t - 1) * 4 + j)
        if t < 3:
            mine[...] = total.astype(BF)
            ring_copy(s, mine, t * 4 + j, step_to(first, sign)).start()
            return
        if j > 0:
            total = total + arrived(12 + j - 1)
        if j < 3:
            mine[...] = total.astype(BF)
            ring_copy(s, mine, 12 + j, step_to(second, sign)).start()
        else:
            gsum[*part(s)] = total

    def xo_rows(way, sub):
        return pl.ds(way * (TOK // 2) + sub * SUB_ROWS, SUB_ROWS)

    def xo_copy(way, sub, t):
        sign = 1 - 2 * way
        rows = xo_rows(way, sub)
        return remote(
            outp.at[ahead("x", sign, 3 - t), rows, :], outr.at[t, rows, :],
            xo_send.at[way, sub, t], xo_recv.at[way, sub, t], step_to("x", sign),
        )

    def xo_step(way, sub, t):
        sign = 1 - 2 * way
        rows = xo_rows(way, sub)
        if t > 0:
            own = ahead("x", sign, 3 - t)
            xo_copy(way, sub, t - 1).wait_recv()
            total = outp[own, rows, :].astype(F32) + outr[t - 1, rows, :].astype(F32)
            if t == 3:
                block_out[rows, :] = total.astype(BF)
                return
            outp[own, rows, :] = total.astype(BF)
        xo_copy(way, sub, t).start()

    ST_AXES = (("y", 4), ("z", 4), ("x", 4), ("c", 2))

    def st_copy(ph, slot, k):
        axis, size = ST_AXES[ph]
        device = {axis: lax.rem(me[axis] + k, size)}
        ref = stat.at[ph, slot]
        return remote(ref, ref, st_send.at[ph, k], st_recv.at[ph, slot], device)

    def st_start(ph, total):
        axis, size = ST_AXES[ph]
        stat[ph, me[axis]] = total
        for k in range(1, size):
            st_copy(ph, me[axis], k).start()

    def st_finish(ph):
        axis, size = ST_AXES[ph]
        for k in range(1, size):
            st_copy(ph, lax.rem(me[axis] + k, size), k).wait_recv()
        total = stat[ph, 0]
        for k in range(1, size):
            total = total + stat[ph, k]
        return total

    def tile(n):
        return pl.ds(pl.multiple_of(n * TILE, TILE), TILE)

    def weights(a, n):
        return full[a, :, :, :, :, tile(n)].reshape(D, TILE)

    def fold(v):
        v = jnp.sum(v.reshape(TOK // 8, 8, TILE), axis=0)
        return v[:, :128] + v[:, 128:]

    def fisher_tile(n):
        product = jnp.dot(xf[0], weights(0, n), preferred_element_type=F32)
        value = ((product * gate[:, tile(n)].astype(F32)) ** 2).astype(BF)
        fish[:, tile(n)] = value
        gate_t[tile(n), :] = jnp.transpose(value)
        acc[0] += fold(value.astype(F32))

    def residual_tile(n):
        residual = jnp.dot(xf[1], weights(1, n), preferred_element_type=F32)
        weighted = fish[:, tile(n)].astype(F32) * residual
        wbuf[:, tile(n)] = weighted.astype(BF)
        acc[1] += fold(weighted * residual)

    def grad_tile(n):
        right = wbuf[:, tile(n)]
        for q in range(4):
            product = jnp.dot(feats_t[q], right, preferred_element_type=F32)
            grad[q, :, :, :, tile(n)] = product.astype(BF).reshape(4, 2, ROWS, TILE)

    def hidden_tile(n):
        product = jnp.dot(xf[1], weights(2, n), preferred_element_type=F32)
        wbuf[:, tile(n)] = (product * gate[:, tile(n)].astype(F32)).astype(BF)

    def out_tile(i):
        target = at("x", 3 - 2 * i + (i // 2) * 3)
        right = full[0, target].reshape(XW, FFP)
        product = lax.dot_general(wbuf[...], right, (((1,), (1,)), ((), ())), preferred_element_type=F32)
        outp[target] = product.astype(BF)

    own_cols = pl.ds(pl.multiple_of(x * XW, XW), XW)
    loads = [
        pltpu.make_async_copy(down_in, down_own, local.at[0]),
        pltpu.make_async_copy(logit_in, logit, local.at[1]),
        pltpu.make_async_copy(offset_in, offset, local.at[2]),
        pltpu.make_async_copy(step_in, step_own, local.at[3]),
        pltpu.make_async_copy(go, xf.at[0, :, own_cols], local.at[4]),
        pltpu.make_async_copy(up_in, up_own, local.at[5]),
        pltpu.make_async_copy(bi, xf.at[1, :, own_cols], local.at[6]),
        pltpu.make_async_copy(gate_in, gate_t.at[pl.ds(0, FF), :], local.at[7]),
    ]
    for load in loads:
        load.start()
    barrier = pltpu.get_barrier_semaphore()
    partners = [{axis: at(axis, k)} for axis in ("z", "y", "x") for k in (1, 2, 3)] + [other]
    for device in partners:
        pl.semaphore_signal(barrier, inc=1, device_id=device, device_id_type=MESH)
    acc[...] = jnp.zeros_like(acc)
    gate_t[FF:, :] = jnp.zeros((FFP - FF, TOK), BF)
    for a in range(3):
        full[a, z, y, c, :, FFP - 128:] = jnp.zeros((ROWS, 128), BF)
    loads[0].wait()
    full[0, z, y, c, :, :FF] = down_own[...]
    for i in (1, 2, 3):
        loads[i].wait()
    soft = jax.nn.sigmoid(logit[...])
    full[1, z, y, c, :, :FF] = (step_own[...] * (soft - offset[...].astype(F32))).astype(BF)
    loads[5].wait()
    full[2, z, y, c, :, :FF] = up_own[...]
    loads[4].wait()
    loads[6].wait()
    pl.semaphore_wait(barrier, len(partners))

    ag_start(0)
    for i in (0, 1):
        x_start(0, i)
    ag_start(1)
    for i in (0, 1):
        x_start(1, i)
    for d in (1, 2, 3):
        ag_first(0, d)
    soft = jax.nn.sigmoid(logit[...])
    centered = 2.0 * soft - 1.0
    sig_slope = soft * (1.0 - soft)
    slope[...] = step_own[...] * sig_slope
    pull[...] = REG_WEIGHT * 8.0 * centered**3 * sig_slope
    reg_sum = jnp.sum(1.0 - (centered * centered) ** 2, axis=(0, 1), keepdims=True)
    acc[2] = jnp.broadcast_to(reg_sum * (1.0 / 1024.0), (8, 128))
    loads[7].wait()


    @pl.loop(0, 3)
    def _(n):
        ag_second(0, n)
        gate[:, tile(n)] = jnp.transpose(gate_t[tile(n), :])

    for i in (0, 1):
        x_wait(0, i)
    for i in (2, 3):
        x_start(0, i)

    @pl.loop(3, 6)
    def _(n):
        ag_second(0, n)
        ag_first(1, n - 2)
        gate[:, tile(n)] = jnp.transpose(gate_t[tile(n), :])

    @pl.loop(6, 10)
    def _(n):
        ag_second(0, n)
        ag_second(1, n - 6)

        @pl.when(n == 6)
        def _():
            gate[:, tile(n)] = jnp.transpose(gate_t[tile(n), :])

    for i in (0, 1):
        x_wait(1, i)
    for i in (2, 3):
        x_start(1, i)

    @pl.loop(10, 12)
    def _(n):
        ag_second(0, n)
        ag_second(1, n - 6)

    ag_start(2)
    for i in (2, 3):
        x_wait(0, i)
    ag_finish(0)

    @pl.loop(0, NT)
    def _(n):
        @pl.when(n < 6)
        def _():
            ag_second(1, n + 6)

        @pl.when((n >= 2) & (n < 5))
        def _():
            ag_first(2, n - 1)

        fisher_tile(n)

    save_fisher = pltpu.make_async_copy(gate_t.at[pl.ds(0, FF), :], fisher_out, local.at[7])
    save_fisher.start()
    ag_second(2, 0)
    for i in (2, 3):
        x_wait(1, i)
    for q in range(4):
        feats_t[q] = jnp.transpose(xf[1, :, q * XW:(q + 1) * XW])
        if q % 2:
            ag_second(2, (q + 1) // 2)
    ag_finish(1)

    def rs_begin(s):
        pair_copy(s).wait_recv()

        @pl.loop(0, 4)
        def _(j):
            rs_step(s, 0, j)

    @pl.loop(0, NT)
    def _(n):
        residual_tile(n)
        ag_second(2, n + 3)
        grad_tile(n)
        for s in range(STREAMS):
            @pl.when(n == READY[s])
            def _():
                pair_copy(s).start()

        for s in EARLY:
            @pl.when(n == READY[s] + 1)
            def _():
                rs_begin(s)

    ag_second(2, 10)
    st_start(0, acc[...])
    for s in LATE:
        rs_begin(s)

    ag_second(2, 11)
    st_start(1, st_finish(0))
    ag_finish(2)

    @pl.loop(0, NT)
    def _(n):
        hidden_tile(n)

        @pl.when((n >= 2) & (n < 6))
        def _():
            for s in range(STREAMS):
                rs_step(s, 1, n - 2)

    st_start(2, st_finish(1))

    def rs_round(t, j):
        for s in range(STREAMS):
            rs_step(s, t, j)

    def xo_round(t, ways=(0, 1)):
        for sub in range(SUBS):
            for way in ways:
                xo_step(way, sub, t)

    @pl.loop(0, 4)
    def _(i):
        out_tile(i)

        @pl.when(i == 0)
        def _():
            xo_round(0, (0,))

        @pl.when(i == 1)
        def _():
            xo_round(0, (1,))

        @pl.when(i < 2)
        def _():
            rs_round(2, 2 * i)
            rs_round(2, 2 * i + 1)

        @pl.when(i == 2)
        def _():
            xo_round(1)
            rs_round(3, 0)

    rs_round(3, 1)
    xo_round(2)
    rs_round(3, 2)
    st_start(3, st_finish(2))
    rs_round(3, 3)
    sums = st_finish(3)
    fisher_sum, recon_sum, reg_sum = (jnp.sum(sums[i], axis=(0, 1), keepdims=True) for i in range(3))
    fisher_mean = fisher_sum / CELLS
    loss_out[...] = recon_sum / (fisher_mean * CELLS) + REG_WEIGHT * reg_sum / WEIGHT_CELLS
    grad_logit[...] = gsum[:, :FF] * (2.0 / fisher_mean) * slope[...] - pull[...]
    xo_round(3)

    for a in range(3):
        ag_drain(a)
    for t in range(2):
        for i in range(4):
            x_copy(t, i, X_MOVES[i][0]).wait_send()
    for s in range(STREAMS):
        pair_copy(s).wait_send()
        ref = ring.at[:, *part(s)]
        remote(ref, ref, rs_send.at[s], rs_recv.at[s, 0], other).wait_send()
    for way in range(2):
        for sub in range(SUBS):
            for t in range(3):
                xo_copy(way, sub, t).wait_send()
    for ph in range(4):
        for k in range(1, ST_AXES[ph][1]):
            st_copy(ph, me[ST_AXES[ph][0]], k).wait_send()
    save_fisher.wait()


def run(*operands):
    vmem, hbm = pl.BlockSpec(memory_space=pltpu.VMEM), pl.BlockSpec(memory_space=pl.ANY)
    dma = pltpu.SemaphoreType.DMA
    return pl.pallas_call(
        kernel,
        out_shape=(
            jax.ShapeDtypeStruct((TOK, XW), BF),
            jax.ShapeDtypeStruct((FF, TOK), BF),
            jax.ShapeDtypeStruct((ROWS, FF), F32),
            jax.ShapeDtypeStruct((1, 1), F32),
        ),
        in_specs=[hbm] * 8,
        out_specs=(vmem, hbm, vmem, vmem),
        scratch_shapes=[
            pltpu.VMEM((3, 4, 4, 2, ROWS, FFP), BF),
            pltpu.VMEM((2, TOK, D), BF),
            pltpu.VMEM((4, XW, TOK), BF),
            pltpu.VMEM((TOK, FFP), BF),
            pltpu.VMEM((FFP, TOK), BF),
            pltpu.VMEM((TOK, FFP), BF),
            pltpu.VMEM((TOK, FFP), BF),
            pltpu.VMEM((4, 4, 2, ROWS, FFP), BF),
            pltpu.VMEM((4, 4, ROWS, FFP), BF),
            pltpu.VMEM((15, ROWS, FFP), BF),
            pltpu.VMEM((4, TOK, XW), BF),
            pltpu.VMEM((3, TOK, XW), BF),
            pltpu.VMEM((3, 8, 128), F32),
            pltpu.VMEM((4, 4, 3, 8, 128), F32),
            pltpu.VMEM((ROWS, FF), BF),
            pltpu.VMEM((ROWS, FF), BF),
            pltpu.VMEM((1, FF), F32),
            pltpu.VMEM((ROWS, FF), F32),
            pltpu.VMEM((ROWS, FF), BF),
            pltpu.VMEM((ROWS, FF), F32),
            pltpu.VMEM((ROWS, FF), F32),
            pltpu.VMEM((ROWS, FFP), F32),
            dma((8,)),
            dma((3, STREAMS, 16)), dma((3, STREAMS)), dma((3, STREAMS, 4)), dma((3, STREAMS)),
            dma((2, 4)), dma((2, 4)),
            dma((STREAMS, 16)), dma((STREAMS,)), dma((STREAMS,)), dma((STREAMS,)),
            dma((2, SUBS, 3)), dma((2, SUBS, 3)),
            dma((4, 4)), dma((4, 4)),
        ],
        compiler_params=pltpu.CompilerParams(
            collective_id=0, has_side_effects=True, vmem_limit_bytes=67043328
        ),
    )(*operands)


def save_kernel(out_in, fisher_in, grad_in, loss_in, out, fisher, grad, loss, out_v, fisher_v, grad_v, loss_v, sems):
    third = FF // 3
    moves = []
    for q in range(3):
        rows = pl.ds(q * third, third)
        moves.append((fisher_in.at[rows, :], fisher_v.at[rows, :], fisher.at[rows, :]))
    moves += [(grad_in, grad_v, grad), (out_in, out_v, out), (loss_in, loss_v, loss)]
    reads = [pltpu.make_async_copy(src, mid, sems.at[0, i]) for i, (src, mid, _) in enumerate(moves)]
    writes = [pltpu.make_async_copy(mid, dst, sems.at[1, i]) for i, (_, mid, dst) in enumerate(moves)]
    for read in reads:
        read.start()
    for read, write in zip(reads, writes):
        read.wait()
        write.start()
    for write in writes:
        write.wait()


def save(*arrays):
    hbm = pl.BlockSpec(memory_space=pl.ANY)
    return pl.pallas_call(
        save_kernel,
        out_shape=tuple(jax.ShapeDtypeStruct(a.shape, a.dtype) for a in arrays),
        in_specs=[hbm] * 4,
        out_specs=(hbm,) * 4,
        scratch_shapes=[pltpu.VMEM(a.shape, a.dtype) for a in arrays] + [pltpu.SemaphoreType.DMA((2, 6))],
    )(*arrays)


def body(
    block_input, gate_act, grad_out, up_weight, down_weight, quant_step, round_logit, grid_offset
):
    block_output, fisher_t, grad_logit, loss = save(*run(
        block_input, gate_act.T, grad_out, up_weight, down_weight.T, quant_step[None, :], round_logit, grid_offset
    ))
    return (block_output, fisher_t.T, grad_logit, loss[0, 0])


def solution(mesh):
    torus = Mesh(mesh.devices.reshape(4, 4, 2, 4), ("z", "y", "c", "x"))
    dp = ("z", "y", "c")
    in_specs = (
        P(dp, "x"), P(dp, "x"), P(dp, "x"), P(dp, "x"), P("x", dp), P("x"), P(dp, "x"), P(dp, "x"),
    )
    out_specs = (P(dp, "x"), P(dp, "x"), P(dp, "x"), P())
    return jax.shard_map(body, mesh=torus, in_specs=in_specs, out_specs=out_specs, check_vma=False)
```

```python
import jax
import jax.numpy as jnp
from jax import lax
from jax.experimental import pallas as pl
from jax.experimental.pallas import tpu as pltpu
from jax.sharding import Mesh
from jax.sharding import PartitionSpec as P

D = 2560
FFW = 6912
TOK = 384
FF = 1728
FFP = 1792
ROWS = 80
XW = 640
TILE = 256
NT = FFP // TILE
REG_WEIGHT = 0.5
CELLS = 12288 * FFW
WEIGHT_CELLS = D * FFW
BF = jnp.bfloat16
F32 = jnp.float32
MESH = pl.DeviceIdType.MESH

GATHER = (("y", "z"), ("z", "y"))
REDUCE = (("z", "y"), ("y", "z"))
SPAN = FFP // 2
READY = (3, 6)
PLACES = (0, -1, 1, 2)
TURNS = (2, 1, -1, 0)
ALL = (0, ROWS)
HALVES = ((0, 48), (48, 32))
SUBS = 3
SUB_ROWS = TOK // SUBS


def kernel(
    bi, gate_in, go, up_in, down_in, step_in, logit_in, offset_in,
    block_out, fisher_out, grad_logit, loss_out,
    full, xf, feats_t, gate, gate_t, fish, wbuf, grad, pair, ring, outp, outr, acc, stat,
    weight_own, step_own, logit, offset, slope, pull,
    local, ag_recv, ag_send, pr_recv, pr_send, x_recv, x_send,
    rs_recv, rs_send, pe_recv, pe_send, xo_recv, xo_send, st_recv, st_send,
):
    me = {name: lax.axis_index(name) for name in ("z", "y", "c", "x")}
    z, y, c, x = me["z"], me["y"], me["c"], me["x"]
    other = {"c": 1 - c}

    def at(axis, k):
        return lax.rem(me[axis] + (k + 4), 4)

    def step_to(axis, sign):
        return {axis: at(axis, sign)}

    def remote(src, dst, send, recv, device):
        return pltpu.make_async_remote_copy(
            src_ref=src, dst_ref=dst, send_sem=send, recv_sem=recv, device_id=device, device_id_type=MESH
        )

    def piece(a, s, d, e, rows):
        first, second = GATHER[s]
        co = {first: at(first, d), second: at(second, e)}
        return full.at[a, co["z"], co["y"], c, pl.ds(*rows), pl.ds(s * SPAN, SPAN)]

    def move(a, s, d, e, rows, axis, sign, slot):
        ref = piece(a, s, d, e, rows)
        remote(ref, ref, ag_send.at[a, s], ag_recv.at[a, s, slot], step_to(axis, sign)).start()

    def wait_piece(a, s, d, e, rows, slot):
        ref = piece(a, s, d, e, rows)
        remote(ref, ref, ag_send.at[a, s], ag_recv.at[a, s, slot], other).wait_recv()

    def along_second(a, s, i):
        for sign, slot in ((1, 0), (-1, 1)):
            move(a, s, PLACES[i], 0, ALL, GATHER[s][1], sign, 4 + 4 * i + slot)

    def forward_second(a, i):
        for s in range(2):
            d, h = PLACES[i], (s + i) % 2
            wait_piece(a, s, d, -1, ALL, 4 + 4 * i)
            move(a, s, d, -1, HALVES[h], GATHER[s][1], 1, 6 + 4 * i)
            wait_piece(a, s, d, 1, ALL, 5 + 4 * i)
            move(a, s, d, 1, HALVES[1 - h], GATHER[s][1], -1, 7 + 4 * i)

    def bundle(a, s, e, parity):
        second = GATHER[s][1]
        cols = pl.ds(s * SPAN, SPAN)
        if second == "z":
            return full.at[a, at("z", e), :, parity, :, cols]
        return full.at[a, :, at("y", e), parity, :, cols]

    def send_pair(a, i):
        for s in range(2):
            ref = bundle(a, s, PLACES[i], c)
            remote(ref, ref, pr_send.at[a, s], pr_recv.at[a, s, i], other).start()

    def ag_start(a):
        for s in range(2):
            for sign, slot in ((1, 0), (-1, 1)):
                move(a, s, 0, 0, ALL, GATHER[s][0], sign, slot)
        for s in range(2):
            along_second(a, s, 0)

    def ag_event(a, k):
        if k == 0:
            for s in range(2):
                first = GATHER[s][0]
                wait_piece(a, s, -1, 0, ALL, 0)
                move(a, s, -1, 0, HALVES[s], first, 1, 2)
                wait_piece(a, s, 1, 0, ALL, 1)
                move(a, s, 1, 0, HALVES[1 - s], first, -1, 3)
            for i in (1, 2):
                for s in range(2):
                    along_second(a, s, i)
        elif k == 1:
            forward_second(a, 0)
        elif k == 2:
            for s in range(2):
                wait_piece(a, s, 2, 0, HALVES[s], 2)
                wait_piece(a, s, 2, 0, HALVES[1 - s], 3)
                along_second(a, s, 3)
            send_pair(a, 0)
        elif k < 6:
            forward_second(a, k - 2)
            if k == 5:
                send_pair(a, 1)
                send_pair(a, 2)
        else:
            for i in range(4):
                for s in range(2):
                    h = (s + i) % 2
                    wait_piece(a, s, PLACES[i], 2, HALVES[h], 6 + 4 * i)
                    wait_piece(a, s, PLACES[i], 2, HALVES[1 - h], 7 + 4 * i)
            send_pair(a, 3)

    def ag_finish(a):
        for s in range(2):
            for i in range(4):
                ref = bundle(a, s, PLACES[i], 1 - c)
                remote(ref, ref, pr_send.at[a, s], pr_recv.at[a, s, i], other).wait_recv()

    def ag_drain(a):
        for s in range(2):
            ref = ring.at[:, :, pl.ds(s * SPAN, SPAN)]
            remote(ref, ref, ag_send.at[a, s], ag_recv.at[a, s, 0], other).wait_send()
            ref = full.at[a, :, :, c, :, pl.ds(s * SPAN, SPAN)]
            remote(ref, ref, pr_send.at[a, s], pr_recv.at[a, s, 0], other).wait_send()

    def x_block(t, k, lo, count):
        return xf.at[t, pl.ds(lo, count), pl.ds(pl.multiple_of(at("x", k) * XW, XW), XW)]

    X_MOVES = ((0, 1, 0, TOK, -1), (0, -1, 0, TOK, 1), (-1, 1, 0, TOK // 2, 2), (1, -1, TOK // 2, TOK // 2, 2))

    def x_copy(t, i, k):
        src, sign, lo, count, got = X_MOVES[i]
        ref = x_block(t, k, lo, count)
        return remote(ref, ref, x_send.at[t, i], x_recv.at[t, i], step_to("x", sign))

    def x_start(t, i):
        x_copy(t, i, X_MOVES[i][0]).start()

    def x_wait(t, i):
        x_copy(t, i, X_MOVES[i][4]).wait_recv()

    def pair_copy(s):
        cols = pl.ds(s * SPAN, SPAN)
        return remote(grad.at[:, :, 1 - c, :, cols], pair.at[:, :, :, cols], pe_send.at[s], pe_recv.at[s], other)

    class Block:
        def __init__(self, s, d, e):
            first, second = REDUCE[s]
            self.s = s
            self.co = {first: at(first, d), second: at(second, e)}

        def ref(self, rows):
            return grad.at[self.co["z"], self.co["y"], c, pl.ds(*rows), pl.ds(self.s * SPAN, SPAN)]

        def sum(self, rows, *slots):
            cols = pl.ds(self.s * SPAN, SPAN)
            total = self.ref(rows)[...].astype(F32)
            total = total + pair[self.co["z"], self.co["y"], pl.ds(*rows), cols].astype(F32)
            for slot in slots:
                total = total + ring[slot, pl.ds(*rows), cols].astype(F32)
            return total

        def copy(self, rows, slot, sem, axis, sign):
            dst = ring.at[slot, pl.ds(*rows), pl.ds(self.s * SPAN, SPAN)]
            device = other if axis is None else step_to(axis, sign)
            return remote(self.ref(rows), dst, rs_send.at[self.s], rs_recv.at[self.s, sem], device)

        def send(self, rows, slot, sem, axis, sign):
            self.copy(rows, slot, sem, axis, sign).start()

        def wait(self, rows, slot, sem):
            self.copy(rows, slot, sem, None, 0).wait_recv()

    def rs_far(s, j):
        first, h = REDUCE[s][0], (s + j) % 2
        block = Block(s, 2, TURNS[j])
        block.ref(ALL)[...] = block.sum(ALL).astype(BF)
        block.send(HALVES[h], j, 4 * j, first, 1)
        block.send(HALVES[1 - h], j, 4 * j + 1, first, -1)

    def rs_near(s, j):
        first = REDUCE[s][0]
        for sign, side in ((1, 0), (-1, 1)):
            h = (s + j + side) % 2
            block = Block(s, sign, TURNS[j])
            block.wait(HALVES[h], j, 4 * j + side)
            rest = block.sum(HALVES[1 - h]).astype(BF)
            block.ref(HALVES[1 - h])[...] = rest
            block.ref(HALVES[h])[...] = block.sum(HALVES[h], j).astype(BF)
            block.send(ALL, 4 + 4 * side + j, 4 * j + 2 + side, first, sign)

    def rs_own(s, j):
        second, h = REDUCE[s][1], s
        block = Block(s, 0, TURNS[j])
        block.wait(ALL, 4 + j, 4 * j + 2)
        block.wait(ALL, 8 + j, 4 * j + 3)
        if j == 0:
            block.ref(ALL)[...] = block.sum(ALL, 4 + j, 8 + j).astype(BF)
            block.send(HALVES[h], 12, 16, second, 1)
            block.send(HALVES[1 - h], 12, 17, second, -1)
        elif j < 3:
            side = j - 1
            h = (h + side) % 2
            block.wait(HALVES[h], 12, 16 + side)
            rest = block.sum(HALVES[1 - h], 4 + j, 8 + j).astype(BF)
            block.ref(HALVES[1 - h])[...] = rest
            block.ref(HALVES[h])[...] = block.sum(HALVES[h], 4 + j, 8 + j, 12).astype(BF)
            block.send(ALL, 13 + side, 18 + side, second, 1 - 2 * side)
        else:
            block.wait(ALL, 13, 18)
            block.wait(ALL, 14, 19)
            total = block.sum(ALL, 4 + j, 8 + j, 13, 14)
            if s == 0:
                logit[:, :SPAN] = total
            else:
                logit[:, SPAN:] = total[:, :FF - SPAN]

    def xo_rows(sub, half=None):
        if half is None:
            return pl.ds(sub * SUB_ROWS, SUB_ROWS)
        return pl.ds(sub * SUB_ROWS + half * (SUB_ROWS // 2), SUB_ROWS // 2)

    def xo_copy(sub, k):
        side, far = k % 2, k < 2
        rows = xo_rows(sub, side if far else None)
        target = at("x", 2 if far else 1 - 2 * side)
        return remote(
            outp.at[target, rows, :], outr.at[0 if far else 1 + side, rows, :],
            xo_send.at[sub, k], xo_recv.at[sub, k], step_to("x", 1 - 2 * side),
        )

    def xo_far(sub):
        for k in (0, 1):
            xo_copy(sub, k).start()

    def xo_near(sub, side):
        target, rows = at("x", 1 - 2 * side), xo_rows(sub, side)
        xo_copy(sub, side).wait_recv()
        total = outp[target, rows, :].astype(F32) + outr[0, rows, :].astype(F32)
        outp[target, rows, :] = total.astype(BF)
        xo_copy(sub, 2 + side).start()

    def xo_own(sub):
        rows = xo_rows(sub)
        for k in (2, 3):
            xo_copy(sub, k).wait_recv()
        total = outp[x, rows, :].astype(F32) + outr[1, rows, :].astype(F32) + outr[2, rows, :].astype(F32)
        block_out[rows, :] = total.astype(BF)

    def xo_all(step, *args):
        for sub in range(SUBS):
            step(sub, *args)

    ST_AXES = (("y", 4), ("z", 4), ("x", 4), ("c", 2))

    def st_copy(ph, slot, k):
        axis, size = ST_AXES[ph]
        device = {axis: lax.rem(me[axis] + k, size)}
        ref = stat.at[ph, slot]
        return remote(ref, ref, st_send.at[ph, k], st_recv.at[ph, slot], device)

    def st_start(ph, total):
        axis, size = ST_AXES[ph]
        stat[ph, me[axis]] = total
        for k in range(1, size):
            st_copy(ph, me[axis], k).start()

    def st_finish(ph):
        axis, size = ST_AXES[ph]
        for k in range(1, size):
            st_copy(ph, lax.rem(me[axis] + k, size), k).wait_recv()
        total = stat[ph, 0]
        for k in range(1, size):
            total = total + stat[ph, k]
        return total

    def tile(n):
        return pl.ds(pl.multiple_of(n * TILE, TILE), TILE)

    def weights(a, n):
        return full[a, :, :, :, :, tile(n)].reshape(D, TILE)

    def fold(v):
        v = jnp.sum(v.reshape(TOK // 8, 8, TILE), axis=0)
        return v[:, :128] + v[:, 128:]

    def fisher_tile(n):
        product = jnp.dot(xf[0], weights(0, n), preferred_element_type=F32)
        value = ((product * gate[:, tile(n)].astype(F32)) ** 2).astype(BF)
        fish[:, tile(n)] = value
        gate_t[tile(n), :] = jnp.transpose(value)
        acc[0] += fold(value.astype(F32))

    def residual_tile(n):
        residual = jnp.dot(xf[1], weights(1, n), preferred_element_type=F32)
        weighted = fish[:, tile(n)].astype(F32) * residual
        wbuf[:, tile(n)] = weighted.astype(BF)
        acc[1] += fold(weighted * residual)

    def grad_tile(n):
        right = wbuf[:, tile(n)]
        for q in range(4):
            product = jnp.dot(feats_t[q], right, preferred_element_type=F32)
            grad[q, :, :, :, tile(n)] = product.astype(BF).reshape(4, 2, ROWS, TILE)

    def hidden_tile(n):
        product = jnp.dot(xf[1], weights(2, n), preferred_element_type=F32)
        wbuf[:, tile(n)] = (product * gate[:, tile(n)].astype(F32)).astype(BF)

    def out_tile(i):
        target = at("x", jnp.where(i == 2, 3, jnp.where(i == 3, 0, 2 - i)))
        right = full[0, target].reshape(XW, FFP)
        product = lax.dot_general(wbuf[...], right, (((1,), (1,)), ((), ())), preferred_element_type=F32)
        outp[target] = product.astype(BF)

    own_cols = pl.ds(pl.multiple_of(x * XW, XW), XW)
    loads = [
        pltpu.make_async_copy(down_in, weight_own, local.at[0]),
        pltpu.make_async_copy(logit_in, logit, local.at[1]),
        pltpu.make_async_copy(offset_in, offset, local.at[2]),
        pltpu.make_async_copy(step_in, step_own, local.at[3]),
        pltpu.make_async_copy(go, xf.at[0, :, own_cols], local.at[4]),
        pltpu.make_async_copy(up_in, weight_own, local.at[5]),
        pltpu.make_async_copy(bi, xf.at[1, :, own_cols], local.at[6]),
        pltpu.make_async_copy(gate_in, gate_t.at[pl.ds(0, FF), :], local.at[7]),
    ]
    for i, load in enumerate(loads):
        if i != 5:
            load.start()
    barrier = pltpu.get_barrier_semaphore()
    partners = [{axis: at(axis, k)} for axis in ("z", "y", "x") for k in (1, 2, 3)] + [other]
    for device in partners:
        pl.semaphore_signal(barrier, inc=1, device_id=device, device_id_type=MESH)
    acc[...] = jnp.zeros_like(acc)
    gate_t[FF:, :] = jnp.zeros((FFP - FF, TOK), BF)
    for a in range(3):
        full[a, z, y, c, :, FFP - 128:] = jnp.zeros((ROWS, 128), BF)
    loads[0].wait()
    full[0, z, y, c, :, :FF] = weight_own[...]
    for i in (1, 2, 3):
        loads[i].wait()
    soft = jax.nn.sigmoid(logit[...])
    full[1, z, y, c, :, :FF] = (step_own[...] * (soft - offset[...].astype(F32))).astype(BF)
    loads[4].wait()
    loads[6].wait()
    pl.semaphore_wait(barrier, len(partners))

    def on(index, value, *calls):
        @pl.when(index == value)
        def _():
            for call, *args in calls:
                call(*args)

    ag_start(0)
    for i in (0, 1):
        x_start(0, i)
    soft = jax.nn.sigmoid(logit[...])
    centered = 2.0 * soft - 1.0
    sig_slope = soft * (1.0 - soft)
    slope[...] = step_own[...] * sig_slope
    pull[...] = REG_WEIGHT * 8.0 * centered**3 * sig_slope
    reg_sum = jnp.sum(1.0 - (centered * centered) ** 2, axis=(0, 1), keepdims=True)
    acc[2] = jnp.broadcast_to(reg_sum * (1.0 / 1024.0), (8, 128))
    loads[7].wait()
    loads[5].start()
    ag_event(0, 0)
    ag_event(0, 1)

    @pl.loop(0, NT)
    def _(n):
        gate[:, tile(n)] = jnp.transpose(gate_t[tile(n), :])
        on(n, 1, (ag_event, 0, 2))
        on(n, 3, (ag_event, 0, 3))
        on(n, 6, (ag_event, 0, 4))

    for i in (0, 1):
        x_wait(0, i)
    for i in (2, 3):
        x_start(0, i)
    for i in (0, 1):
        x_start(1, i)
    loads[5].wait()
    full[2, z, y, c, :, :FF] = weight_own[...]
    ag_event(0, 5)
    ag_start(1)
    ag_event(0, 6)
    for i in (2, 3):
        x_wait(0, i)
    ag_finish(0)

    @pl.loop(0, NT)
    def _(n):
        for k in range(5):
            on(n, k + 1, (ag_event, 1, k))
        fisher_tile(n)

    save_fisher = pltpu.make_async_copy(gate_t.at[pl.ds(0, FF), :], fisher_out, local.at[7])
    save_fisher.start()
    for i in (0, 1):
        x_wait(1, i)
    for i in (2, 3):
        x_start(1, i)
    ag_event(1, 5)
    ag_start(2)
    ag_event(1, 6)
    for i in (2, 3):
        x_wait(1, i)
    for q in range(4):
        feats_t[q] = jnp.transpose(xf[1, :, q * XW:(q + 1) * XW])
    ag_finish(1)

    @pl.loop(0, NT)
    def _(n):
        residual_tile(n)
        for k in range(6):
            on(n, k, (ag_event, 2, k))
        grad_tile(n)
        on(n, READY[0], (lambda: pair_copy(0).start(),))
        on(n, READY[1], (lambda: pair_copy(1).start(),))
        on(n, 5, (lambda: pair_copy(0).wait_recv(),), (rs_far, 0, 0), (rs_far, 0, 1))
        on(n, 6, (rs_near, 0, 0), (rs_far, 0, 2), (rs_near, 0, 1), (rs_far, 0, 3))

    st_start(0, acc[...])
    ag_event(2, 6)
    rs_near(0, 2)
    pair_copy(1).wait_recv()
    rs_far(1, 0)
    rs_far(1, 1)
    rs_near(0, 3)
    ag_finish(2)
    st_start(1, st_finish(0))

    @pl.loop(0, NT)
    def _(n):
        hidden_tile(n)
        on(n, 1, (rs_own, 0, 0))
        on(n, 3, (rs_near, 1, 0), (rs_far, 1, 2))
        on(n, 5, (rs_near, 1, 1), (rs_far, 1, 3))
        on(n, 6, (rs_own, 0, 1), (rs_own, 0, 2))

    st_start(2, st_finish(1))

    @pl.loop(0, 4)
    def _(i):
        out_tile(i)
        on(i, 0, (xo_all, xo_far), (rs_near, 1, 2), (rs_own, 1, 0))
        on(i, 1, (rs_near, 1, 3), (rs_own, 0, 3))
        on(i, 2, (xo_all, xo_near, 0), (xo_all, xo_near, 1), (rs_own, 1, 1))
        on(i, 3, (rs_own, 1, 2))

    st_start(3, st_finish(2))
    rs_own(1, 3)
    sums = st_finish(3)
    fisher_sum, recon_sum, reg_sum = (jnp.sum(sums[i], axis=(0, 1), keepdims=True) for i in range(3))
    fisher_mean = fisher_sum / CELLS
    loss_out[...] = recon_sum / (fisher_mean * CELLS) + REG_WEIGHT * reg_sum / WEIGHT_CELLS
    grad_logit[...] = logit[...] * (2.0 / fisher_mean) * slope[...] - pull[...]
    xo_all(xo_own)

    for a in range(3):
        ag_drain(a)
    for t in range(2):
        for i in range(4):
            x_copy(t, i, X_MOVES[i][0]).wait_send()
    for s in range(2):
        pair_copy(s).wait_send()
        ref = ring.at[:, :, pl.ds(s * SPAN, SPAN)]
        remote(ref, ref, rs_send.at[s], rs_recv.at[s, 0], other).wait_send()
    for sub in range(SUBS):
        for k in range(4):
            xo_copy(sub, k).wait_send()
    for ph in range(4):
        for k in range(1, ST_AXES[ph][1]):
            st_copy(ph, me[ST_AXES[ph][0]], k).wait_send()
    save_fisher.wait()


def run(*operands):
    vmem, hbm = pl.BlockSpec(memory_space=pltpu.VMEM), pl.BlockSpec(memory_space=pl.ANY)
    dma = pltpu.SemaphoreType.DMA
    return pl.pallas_call(
        kernel,
        out_shape=(
            jax.ShapeDtypeStruct((TOK, XW), BF),
            jax.ShapeDtypeStruct((FF, TOK), BF),
            jax.ShapeDtypeStruct((ROWS, FF), F32),
            jax.ShapeDtypeStruct((1, 1), F32),
        ),
        in_specs=[hbm] * 8,
        out_specs=(vmem, hbm, vmem, vmem),
        scratch_shapes=[
            pltpu.VMEM((3, 4, 4, 2, ROWS, FFP), BF),
            pltpu.VMEM((2, TOK, D), BF),
            pltpu.VMEM((4, XW, TOK), BF),
            pltpu.VMEM((TOK, FFP), BF),
            pltpu.VMEM((FFP, TOK), BF),
            pltpu.VMEM((TOK, FFP), BF),
            pltpu.VMEM((TOK, FFP), BF),
            pltpu.VMEM((4, 4, 2, ROWS, FFP), BF),
            pltpu.VMEM((4, 4, ROWS, FFP), BF),
            pltpu.VMEM((15, ROWS, FFP), BF),
            pltpu.VMEM((4, TOK, XW), BF),
            pltpu.VMEM((3, TOK, XW), BF),
            pltpu.VMEM((3, 8, 128), F32),
            pltpu.VMEM((4, 4, 3, 8, 128), F32),
            pltpu.VMEM((ROWS, FF), BF),
            pltpu.VMEM((1, FF), F32),
            pltpu.VMEM((ROWS, FF), F32),
            pltpu.VMEM((ROWS, FF), BF),
            pltpu.VMEM((ROWS, FF), F32),
            pltpu.VMEM((ROWS, FF), F32),
            dma((8,)),
            dma((3, 2, 20)), dma((3, 2)), dma((3, 2, 4)), dma((3, 2)),
            dma((2, 4)), dma((2, 4)),
            dma((2, 20)), dma((2,)), dma((2,)), dma((2,)),
            dma((SUBS, 4)), dma((SUBS, 4)),
            dma((4, 4)), dma((4, 4)),
        ],
        compiler_params=pltpu.CompilerParams(
            collective_id=0, has_side_effects=True, vmem_limit_bytes=67043328
        ),
    )(*operands)


def save_kernel(out_in, fisher_in, grad_in, loss_in, out, fisher, grad, loss, out_v, fisher_v, grad_v, loss_v, sems):
    third = FF // 3
    moves = []
    for q in range(3):
        rows = pl.ds(q * third, third)
        moves.append((fisher_in.at[rows, :], fisher_v.at[rows, :], fisher.at[rows, :]))
    moves += [(grad_in, grad_v, grad), (out_in, out_v, out), (loss_in, loss_v, loss)]
    reads = [pltpu.make_async_copy(src, mid, sems.at[0, i]) for i, (src, mid, _) in enumerate(moves)]
    writes = [pltpu.make_async_copy(mid, dst, sems.at[1, i]) for i, (_, mid, dst) in enumerate(moves)]
    for read in reads:
        read.start()
    for read, write in zip(reads, writes):
        read.wait()
        write.start()
    for write in writes:
        write.wait()


def save(*arrays):
    hbm = pl.BlockSpec(memory_space=pl.ANY)
    return pl.pallas_call(
        save_kernel,
        out_shape=tuple(jax.ShapeDtypeStruct(a.shape, a.dtype) for a in arrays),
        in_specs=[hbm] * 4,
        out_specs=(hbm,) * 4,
        scratch_shapes=[pltpu.VMEM(a.shape, a.dtype) for a in arrays] + [pltpu.SemaphoreType.DMA((2, 6))],
    )(*arrays)


def body(
    block_input, gate_act, grad_out, up_weight, down_weight, quant_step, round_logit, grid_offset
):
    block_output, fisher_t, grad_logit, loss = save(*run(
        block_input, gate_act.T, grad_out, up_weight, down_weight.T, quant_step[None, :], round_logit, grid_offset
    ))
    return (block_output, fisher_t.T, grad_logit, loss[0, 0])


def solution(mesh):
    torus = Mesh(mesh.devices.reshape(4, 4, 2, 4), ("z", "y", "c", "x"))
    dp = ("z", "y", "c")
    in_specs = (
        P(dp, "x"), P(dp, "x"), P(dp, "x"), P(dp, "x"), P("x", dp), P("x"), P(dp, "x"), P(dp, "x"),
    )
    out_specs = (P(dp, "x"), P(dp, "x"), P(dp, "x"), P())
    return jax.shard_map(body, mesh=torus, in_specs=in_specs, out_specs=out_specs, check_vma=False)
```

```python
import jax
import jax.numpy as jnp
from jax import lax
from jax.experimental import pallas as pl
from jax.experimental.pallas import tpu as pltpu
from jax.sharding import Mesh
from jax.sharding import PartitionSpec as P

D = 2560
FFW = 6912
TOK = 384
FF = 1728
FFP = 1792
ROWS = 80
XW = 640
TILE = 256
NT = FFP // TILE
REG_WEIGHT = 0.5
CELLS = 12288 * FFW
WEIGHT_CELLS = D * FFW
BF = jnp.bfloat16
F32 = jnp.float32
MESH = pl.DeviceIdType.MESH

GATHER = (("y", "z"), ("z", "y"))
REDUCE = (("z", "y"), ("y", "z"))
SPAN = FFP // 2
READY = (3, 6)
PLACES = (0, -1, 1, 2)
TURNS = (2, 1, -1, 0)
ALL = (0, ROWS)
HALVES = ((0, 48), (48, 32))
SUBS = 3
SUB_ROWS = TOK // SUBS


def kernel(
    bi, gate_in, go, up_in, down_in, step_in, logit_in, offset_in,
    block_out, fisher_out, grad_logit, loss_out,
    full, xf, feats_t, gate, gate_t, fish, wbuf, grad, pair, ring, outp, outr, acc, stat,
    weight_own, step_own, logit, offset, slope, pull,
    local, ag_recv, ag_send, pr_recv, pr_send, x_recv, x_send,
    rs_recv, rs_send, pe_recv, pe_send, xo_recv, xo_send, st_recv, st_send,
):
    me = {name: lax.axis_index(name) for name in ("z", "y", "c", "x")}
    z, y, c, x = me["z"], me["y"], me["c"], me["x"]
    other = {"c": 1 - c}

    def at(axis, k):
        return lax.rem(me[axis] + (k + 4), 4)

    def step_to(axis, sign):
        return {axis: at(axis, sign)}

    def remote(src, dst, send, recv, device):
        return pltpu.make_async_remote_copy(
            src_ref=src, dst_ref=dst, send_sem=send, recv_sem=recv, device_id=device, device_id_type=MESH
        )

    def piece(a, s, d, e, rows):
        first, second = GATHER[s]
        co = {first: at(first, d), second: at(second, e)}
        return full.at[a, co["z"], co["y"], c, pl.ds(*rows), pl.ds(s * SPAN, SPAN)]

    def move(a, s, d, e, rows, axis, sign, slot):
        ref = piece(a, s, d, e, rows)
        remote(ref, ref, ag_send.at[a, s], ag_recv.at[a, s, slot], step_to(axis, sign)).start()

    def wait_piece(a, s, d, e, rows, slot):
        ref = piece(a, s, d, e, rows)
        remote(ref, ref, ag_send.at[a, s], ag_recv.at[a, s, slot], other).wait_recv()

    def along_second(a, s, i):
        for sign, slot in ((1, 0), (-1, 1)):
            move(a, s, PLACES[i], 0, ALL, GATHER[s][1], sign, 4 + 4 * i + slot)

    def forward_second(a, i):
        for s in range(2):
            d, h = PLACES[i], (s + i) % 2
            wait_piece(a, s, d, -1, ALL, 4 + 4 * i)
            move(a, s, d, -1, HALVES[h], GATHER[s][1], 1, 6 + 4 * i)
            wait_piece(a, s, d, 1, ALL, 5 + 4 * i)
            move(a, s, d, 1, HALVES[1 - h], GATHER[s][1], -1, 7 + 4 * i)

    def bundle(a, s, e, parity):
        second = GATHER[s][1]
        cols = pl.ds(s * SPAN, SPAN)
        if second == "z":
            return full.at[a, at("z", e), :, parity, :, cols]
        return full.at[a, :, at("y", e), parity, :, cols]

    def send_pair(a, i):
        for s in range(2):
            ref = bundle(a, s, PLACES[i], c)
            remote(ref, ref, pr_send.at[a, s], pr_recv.at[a, s, i], other).start()

    def ag_start(a):
        for s in range(2):
            for sign, slot in ((1, 0), (-1, 1)):
                move(a, s, 0, 0, ALL, GATHER[s][0], sign, slot)
        for s in range(2):
            along_second(a, s, 0)

    def ag_event(a, k):
        if k == 0:
            for s in range(2):
                first = GATHER[s][0]
                wait_piece(a, s, -1, 0, ALL, 0)
                move(a, s, -1, 0, HALVES[s], first, 1, 2)
                wait_piece(a, s, 1, 0, ALL, 1)
                move(a, s, 1, 0, HALVES[1 - s], first, -1, 3)
            for i in (1, 2):
                for s in range(2):
                    along_second(a, s, i)
        elif k == 1:
            forward_second(a, 0)
        elif k == 2:
            for s in range(2):
                wait_piece(a, s, 2, 0, HALVES[s], 2)
                wait_piece(a, s, 2, 0, HALVES[1 - s], 3)
                along_second(a, s, 3)
            send_pair(a, 0)
        elif k < 6:
            forward_second(a, k - 2)
            if k == 5:
                send_pair(a, 1)
                send_pair(a, 2)
        else:
            for i in range(4):
                for s in range(2):
                    h = (s + i) % 2
                    wait_piece(a, s, PLACES[i], 2, HALVES[h], 6 + 4 * i)
                    wait_piece(a, s, PLACES[i], 2, HALVES[1 - h], 7 + 4 * i)
            send_pair(a, 3)

    def ag_finish(a):
        for s in range(2):
            for i in range(4):
                ref = bundle(a, s, PLACES[i], 1 - c)
                remote(ref, ref, pr_send.at[a, s], pr_recv.at[a, s, i], other).wait_recv()

    def ag_drain(a):
        for s in range(2):
            ref = ring.at[:, :, pl.ds(s * SPAN, SPAN)]
            remote(ref, ref, ag_send.at[a, s], ag_recv.at[a, s, 0], other).wait_send()
            ref = full.at[a, :, :, c, :, pl.ds(s * SPAN, SPAN)]
            remote(ref, ref, pr_send.at[a, s], pr_recv.at[a, s, 0], other).wait_send()

    def x_block(t, k, lo, count):
        return xf.at[t, pl.ds(lo, count), pl.ds(pl.multiple_of(at("x", k) * XW, XW), XW)]

    X_MOVES = ((0, 1, 0, TOK, -1), (0, -1, 0, TOK, 1), (-1, 1, 0, TOK // 2, 2), (1, -1, TOK // 2, TOK // 2, 2))

    def x_copy(t, i, k):
        src, sign, lo, count, got = X_MOVES[i]
        ref = x_block(t, k, lo, count)
        return remote(ref, ref, x_send.at[t, i], x_recv.at[t, i], step_to("x", sign))

    def x_start(t, i):
        x_copy(t, i, X_MOVES[i][0]).start()

    def x_wait(t, i):
        x_copy(t, i, X_MOVES[i][4]).wait_recv()

    def pair_copy(s):
        cols = pl.ds(s * SPAN, SPAN)
        return remote(grad.at[:, :, 1 - c, :, cols], pair.at[:, :, :, cols], pe_send.at[s], pe_recv.at[s], other)

    class Block:
        def __init__(self, s, d, e):
            first, second = REDUCE[s]
            self.s = s
            self.co = {first: at(first, d), second: at(second, e)}

        def ref(self, rows):
            return grad.at[self.co["z"], self.co["y"], c, pl.ds(*rows), pl.ds(self.s * SPAN, SPAN)]

        def sum(self, rows, *slots):
            cols = pl.ds(self.s * SPAN, SPAN)
            total = self.ref(rows)[...].astype(F32)
            total = total + pair[self.co["z"], self.co["y"], pl.ds(*rows), cols].astype(F32)
            for slot in slots:
                total = total + ring[slot, pl.ds(*rows), cols].astype(F32)
            return total

        def copy(self, rows, slot, sem, axis, sign):
            dst = ring.at[slot, pl.ds(*rows), pl.ds(self.s * SPAN, SPAN)]
            device = other if axis is None else step_to(axis, sign)
            return remote(self.ref(rows), dst, rs_send.at[self.s], rs_recv.at[self.s, sem], device)

        def send(self, rows, slot, sem, axis, sign):
            self.copy(rows, slot, sem, axis, sign).start()

        def wait(self, rows, slot, sem):
            self.copy(rows, slot, sem, None, 0).wait_recv()

    def rs_far(s, j):
        first, h = REDUCE[s][0], (s + j) % 2
        block = Block(s, 2, TURNS[j])
        block.ref(ALL)[...] = block.sum(ALL).astype(BF)
        block.send(HALVES[h], j, 4 * j, first, 1)
        block.send(HALVES[1 - h], j, 4 * j + 1, first, -1)

    def rs_near(s, j):
        first = REDUCE[s][0]
        for sign, side in ((1, 0), (-1, 1)):
            h = (s + j + side) % 2
            block = Block(s, sign, TURNS[j])
            block.wait(HALVES[h], j, 4 * j + side)
            rest = block.sum(HALVES[1 - h]).astype(BF)
            block.ref(HALVES[1 - h])[...] = rest
            block.ref(HALVES[h])[...] = block.sum(HALVES[h], j).astype(BF)
            block.send(ALL, 4 + 4 * side + j, 4 * j + 2 + side, first, sign)

    def rs_own(s, j):
        second, h = REDUCE[s][1], s
        block = Block(s, 0, TURNS[j])
        block.wait(ALL, 4 + j, 4 * j + 2)
        block.wait(ALL, 8 + j, 4 * j + 3)
        if j == 0:
            block.ref(ALL)[...] = block.sum(ALL, 4 + j, 8 + j).astype(BF)
            block.send(HALVES[h], 12, 16, second, 1)
            block.send(HALVES[1 - h], 12, 17, second, -1)
        elif j < 3:
            side = j - 1
            h = (h + side) % 2
            block.wait(HALVES[h], 12, 16 + side)
            rest = block.sum(HALVES[1 - h], 4 + j, 8 + j).astype(BF)
            block.ref(HALVES[1 - h])[...] = rest
            block.ref(HALVES[h])[...] = block.sum(HALVES[h], 4 + j, 8 + j, 12).astype(BF)
            block.send(ALL, 13 + side, 18 + side, second, 1 - 2 * side)
        else:
            block.wait(ALL, 13, 18)
            block.wait(ALL, 14, 19)
            total = block.sum(ALL, 4 + j, 8 + j, 13, 14)
            if s == 0:
                logit[:, :SPAN] = total
            else:
                logit[:, SPAN:] = total[:, :FF - SPAN]

    def xo_rows(sub, half=None):
        if half is None:
            return pl.ds(sub * SUB_ROWS, SUB_ROWS)
        return pl.ds(sub * SUB_ROWS + half * (SUB_ROWS // 2), SUB_ROWS // 2)

    def xo_copy(sub, k):
        side, far = k % 2, k < 2
        rows = xo_rows(sub, side if far else None)
        target = at("x", 2 if far else 1 - 2 * side)
        return remote(
            outp.at[target, rows, :], outr.at[0 if far else 1 + side, rows, :],
            xo_send.at[sub, k], xo_recv.at[sub, k], step_to("x", 1 - 2 * side),
        )

    def xo_far(sub):
        for k in (0, 1):
            xo_copy(sub, k).start()

    def xo_near(sub, side):
        target, rows = at("x", 1 - 2 * side), xo_rows(sub, side)
        xo_copy(sub, side).wait_recv()
        total = outp[target, rows, :].astype(F32) + outr[0, rows, :].astype(F32)
        outp[target, rows, :] = total.astype(BF)
        xo_copy(sub, 2 + side).start()

    def xo_own(sub):
        rows = xo_rows(sub)
        for k in (2, 3):
            xo_copy(sub, k).wait_recv()
        total = outp[x, rows, :].astype(F32) + outr[1, rows, :].astype(F32) + outr[2, rows, :].astype(F32)
        block_out[rows, :] = total.astype(BF)

    def xo_all(step, *args):
        for sub in range(SUBS):
            step(sub, *args)

    ST_AXES = (("y", 4), ("z", 4), ("x", 4), ("c", 2))

    def st_copy(ph, slot, k):
        axis, size = ST_AXES[ph]
        device = {axis: lax.rem(me[axis] + k, size)}
        ref = stat.at[ph, slot]
        return remote(ref, ref, st_send.at[ph, k], st_recv.at[ph, slot], device)

    def st_start(ph, total):
        axis, size = ST_AXES[ph]
        stat[ph, me[axis]] = total
        for k in range(1, size):
            st_copy(ph, me[axis], k).start()

    def st_finish(ph):
        axis, size = ST_AXES[ph]
        for k in range(1, size):
            st_copy(ph, lax.rem(me[axis] + k, size), k).wait_recv()
        total = stat[ph, 0]
        for k in range(1, size):
            total = total + stat[ph, k]
        return total

    def tile(n):
        return pl.ds(pl.multiple_of(n * TILE, TILE), TILE)

    def weights(a, n):
        return full[a, :, :, :, :, tile(n)].reshape(D, TILE)

    def fold(v):
        v = jnp.sum(v.reshape(TOK // 8, 8, TILE), axis=0)
        return v[:, :128] + v[:, 128:]

    def fisher_tile(n):
        product = jnp.dot(xf[0], weights(0, n), preferred_element_type=F32)
        value = ((product * gate[:, tile(n)].astype(F32)) ** 2).astype(BF)
        fish[:, tile(n)] = value
        gate_t[tile(n), :] = jnp.transpose(value)
        acc[0] += fold(value.astype(F32))

    def residual_tile(n):
        residual = jnp.dot(xf[1], weights(1, n), preferred_element_type=F32)
        weighted = fish[:, tile(n)].astype(F32) * residual
        wbuf[:, tile(n)] = weighted.astype(BF)
        acc[1] += fold(weighted * residual)

    def grad_tile(n):
        right = wbuf[:, tile(n)]
        for q in range(4):
            product = jnp.dot(feats_t[q], right, preferred_element_type=F32)
            grad[q, :, :, :, tile(n)] = product.astype(BF).reshape(4, 2, ROWS, TILE)

    def hidden_tile(n):
        product = jnp.dot(xf[1], weights(2, n), preferred_element_type=F32)
        wbuf[:, tile(n)] = (product * gate[:, tile(n)].astype(F32)).astype(BF)

    def out_tile(i):
        target = at("x", jnp.where(i == 2, 3, jnp.where(i == 3, 0, 2 - i)))
        right = full[0, target].reshape(XW, FFP)
        product = lax.dot_general(wbuf[...], right, (((1,), (1,)), ((), ())), preferred_element_type=F32)
        outp[target] = product.astype(BF)

    own_cols = pl.ds(pl.multiple_of(x * XW, XW), XW)
    loads = [
        pltpu.make_async_copy(down_in, weight_own, local.at[0]),
        pltpu.make_async_copy(logit_in, logit, local.at[1]),
        pltpu.make_async_copy(offset_in, offset, local.at[2]),
        pltpu.make_async_copy(step_in, step_own, local.at[3]),
        pltpu.make_async_copy(go, xf.at[0, :, own_cols], local.at[4]),
        pltpu.make_async_copy(up_in, weight_own, local.at[5]),
        pltpu.make_async_copy(bi, xf.at[1, :, own_cols], local.at[6]),
        pltpu.make_async_copy(gate_in, gate_t.at[pl.ds(0, FF), :], local.at[7]),
    ]
    for i, load in enumerate(loads):
        if i != 5:
            load.start()
    barrier = pltpu.get_barrier_semaphore()
    partners = [{axis: at(axis, k)} for axis in ("z", "y", "x") for k in (1, 2, 3)] + [other]
    for device in partners:
        pl.semaphore_signal(barrier, inc=1, device_id=device, device_id_type=MESH)
    acc[...] = jnp.zeros_like(acc)
    gate_t[FF:, :] = jnp.zeros((FFP - FF, TOK), BF)
    for a in range(3):
        full[a, z, y, c, :, FFP - 128:] = jnp.zeros((ROWS, 128), BF)
    loads[0].wait()
    full[0, z, y, c, :, :FF] = weight_own[...]
    for i in (1, 2, 3):
        loads[i].wait()
    soft = jax.nn.sigmoid(logit[...])
    full[1, z, y, c, :, :FF] = (step_own[...] * (soft - offset[...].astype(F32))).astype(BF)
    loads[4].wait()
    loads[6].wait()
    pl.semaphore_wait(barrier, len(partners))

    def on(index, value, *calls):
        @pl.when(index == value)
        def _():
            for call, *args in calls:
                call(*args)

    ag_start(0)
    for i in (0, 1):
        x_start(0, i)
    soft = jax.nn.sigmoid(logit[...])
    centered = 2.0 * soft - 1.0
    sig_slope = soft * (1.0 - soft)
    slope[...] = step_own[...] * sig_slope
    pull[...] = REG_WEIGHT * 8.0 * centered**3 * sig_slope
    reg_sum = jnp.sum(1.0 - (centered * centered) ** 2, axis=(0, 1), keepdims=True)
    acc[2] = jnp.broadcast_to(reg_sum * (1.0 / 1024.0), (8, 128))
    loads[7].wait()
    loads[5].start()
    ag_event(0, 0)
    ag_event(0, 1)

    @pl.loop(0, NT)
    def _(n):
        gate[:, tile(n)] = jnp.transpose(gate_t[tile(n), :])
        on(n, 1, (ag_event, 0, 2))
        on(n, 3, (ag_event, 0, 3))
        on(n, 6, (ag_event, 0, 4))

    for i in (0, 1):
        x_wait(0, i)
    for i in (2, 3):
        x_start(0, i)
    for i in (0, 1):
        x_start(1, i)
    loads[5].wait()
    full[2, z, y, c, :, :FF] = weight_own[...]
    ag_event(0, 5)
    ag_start(1)
    ag_event(0, 6)
    for i in (2, 3):
        x_wait(0, i)
    ag_finish(0)

    @pl.loop(0, NT)
    def _(n):
        for k in range(5):
            on(n, k + 1, (ag_event, 1, k))
        on(n, 4, (x_wait, 1, 0), (x_wait, 1, 1), (x_start, 1, 2), (x_start, 1, 3))
        fisher_tile(n)

    save_fisher = pltpu.make_async_copy(gate_t.at[pl.ds(0, FF), :], fisher_out, local.at[7])
    save_fisher.start()
    ag_event(1, 5)
    ag_start(2)
    for i in (2, 3):
        x_wait(1, i)
    for q in range(4):
        feats_t[q] = jnp.transpose(xf[1, :, q * XW:(q + 1) * XW])
    ag_event(1, 6)
    ag_finish(1)

    @pl.loop(0, NT)
    def _(n):
        residual_tile(n)
        for k in range(6):
            on(n, k, (ag_event, 2, k))
        grad_tile(n)
        on(n, READY[0], (lambda: pair_copy(0).start(),))
        on(n, READY[1], (lambda: pair_copy(1).start(),))
        on(n, 5, (lambda: pair_copy(0).wait_recv(),), *((rs_far, 0, j) for j in range(4)))

    st_start(0, acc[...])
    ag_event(2, 6)
    ag_finish(2)

    @pl.loop(0, NT)
    def _(n):
        hidden_tile(n)
        on(n, 0, (rs_near, 0, 0))
        on(
            n, 1, (rs_near, 0, 1), (lambda: pair_copy(1).wait_recv(),), (rs_far, 1, 0), (rs_far, 1, 1),
            (rs_near, 0, 2), (rs_far, 1, 2), (rs_far, 1, 3),
        )
        on(n, 2, (rs_near, 0, 3))
        on(n, 3, (lambda: st_start(1, st_finish(0)),))
        on(n, 4, (rs_own, 0, 0), (rs_near, 1, 0), (rs_near, 1, 1))
        on(n, 6, (rs_near, 1, 2))

    st_start(2, st_finish(1))

    @pl.loop(0, 4)
    def _(i):
        out_tile(i)
        on(i, 0, (xo_all, xo_far), (rs_own, 0, 1), (rs_own, 0, 2), (rs_near, 1, 3))
        on(i, 1, (rs_own, 1, 0), (lambda: st_start(3, st_finish(2)),))
        on(i, 2, (xo_all, xo_near, 0), (xo_all, xo_near, 1))
        on(i, 3, (rs_own, 1, 1), (rs_own, 1, 2))

    rs_own(0, 3)
    rs_own(1, 3)
    sums = st_finish(3)
    fisher_sum, recon_sum, reg_sum = (jnp.sum(sums[i], axis=(0, 1), keepdims=True) for i in range(3))
    fisher_mean = fisher_sum / CELLS
    loss_out[...] = recon_sum / (fisher_mean * CELLS) + REG_WEIGHT * reg_sum / WEIGHT_CELLS
    grad_logit[...] = logit[...] * (2.0 / fisher_mean) * slope[...] - pull[...]
    xo_all(xo_own)

    for a in range(3):
        ag_drain(a)
    for t in range(2):
        for i in range(4):
            x_copy(t, i, X_MOVES[i][0]).wait_send()
    for s in range(2):
        pair_copy(s).wait_send()
        ref = ring.at[:, :, pl.ds(s * SPAN, SPAN)]
        remote(ref, ref, rs_send.at[s], rs_recv.at[s, 0], other).wait_send()
    for sub in range(SUBS):
        for k in range(4):
            xo_copy(sub, k).wait_send()
    for ph in range(4):
        for k in range(1, ST_AXES[ph][1]):
            st_copy(ph, me[ST_AXES[ph][0]], k).wait_send()
    save_fisher.wait()


def run(*operands):
    vmem, hbm = pl.BlockSpec(memory_space=pltpu.VMEM), pl.BlockSpec(memory_space=pl.ANY)
    dma = pltpu.SemaphoreType.DMA
    return pl.pallas_call(
        kernel,
        out_shape=(
            jax.ShapeDtypeStruct((TOK, XW), BF),
            jax.ShapeDtypeStruct((FF, TOK), BF),
            jax.ShapeDtypeStruct((ROWS, FF), F32),
            jax.ShapeDtypeStruct((1, 1), F32),
        ),
        in_specs=[hbm] * 8,
        out_specs=(vmem, hbm, vmem, vmem),
        scratch_shapes=[
            pltpu.VMEM((3, 4, 4, 2, ROWS, FFP), BF),
            pltpu.VMEM((2, TOK, D), BF),
            pltpu.VMEM((4, XW, TOK), BF),
            pltpu.VMEM((TOK, FFP), BF),
            pltpu.VMEM((FFP, TOK), BF),
            pltpu.VMEM((TOK, FFP), BF),
            pltpu.VMEM((TOK, FFP), BF),
            pltpu.VMEM((4, 4, 2, ROWS, FFP), BF),
            pltpu.VMEM((4, 4, ROWS, FFP), BF),
            pltpu.VMEM((15, ROWS, FFP), BF),
            pltpu.VMEM((4, TOK, XW), BF),
            pltpu.VMEM((3, TOK, XW), BF),
            pltpu.VMEM((3, 8, 128), F32),
            pltpu.VMEM((4, 4, 3, 8, 128), F32),
            pltpu.VMEM((ROWS, FF), BF),
            pltpu.VMEM((1, FF), F32),
            pltpu.VMEM((ROWS, FF), F32),
            pltpu.VMEM((ROWS, FF), BF),
            pltpu.VMEM((ROWS, FF), F32),
            pltpu.VMEM((ROWS, FF), F32),
            dma((8,)),
            dma((3, 2, 20)), dma((3, 2)), dma((3, 2, 4)), dma((3, 2)),
            dma((2, 4)), dma((2, 4)),
            dma((2, 20)), dma((2,)), dma((2,)), dma((2,)),
            dma((SUBS, 4)), dma((SUBS, 4)),
            dma((4, 4)), dma((4, 4)),
        ],
        compiler_params=pltpu.CompilerParams(
            collective_id=0, has_side_effects=True, vmem_limit_bytes=67043328
        ),
    )(*operands)


def save_kernel(out_in, fisher_in, grad_in, loss_in, out, fisher, grad, loss, out_v, fisher_v, grad_v, loss_v, sems):
    third = FF // 3
    moves = []
    for q in range(3):
        rows = pl.ds(q * third, third)
        moves.append((fisher_in.at[rows, :], fisher_v.at[rows, :], fisher.at[rows, :]))
    moves += [(grad_in, grad_v, grad), (out_in, out_v, out), (loss_in, loss_v, loss)]
    reads = [pltpu.make_async_copy(src, mid, sems.at[0, i]) for i, (src, mid, _) in enumerate(moves)]
    writes = [pltpu.make_async_copy(mid, dst, sems.at[1, i]) for i, (_, mid, dst) in enumerate(moves)]
    for read in reads:
        read.start()
    for read, write in zip(reads, writes):
        read.wait()
        write.start()
    for write in writes:
        write.wait()


def save(*arrays):
    hbm = pl.BlockSpec(memory_space=pl.ANY)
    return pl.pallas_call(
        save_kernel,
        out_shape=tuple(jax.ShapeDtypeStruct(a.shape, a.dtype) for a in arrays),
        in_specs=[hbm] * 4,
        out_specs=(hbm,) * 4,
        scratch_shapes=[pltpu.VMEM(a.shape, a.dtype) for a in arrays] + [pltpu.SemaphoreType.DMA((2, 6))],
    )(*arrays)


def body(
    block_input, gate_act, grad_out, up_weight, down_weight, quant_step, round_logit, grid_offset
):
    block_output, fisher_t, grad_logit, loss = save(*run(
        block_input, gate_act.T, grad_out, up_weight, down_weight.T, quant_step[None, :], round_logit, grid_offset
    ))
    return (block_output, fisher_t.T, grad_logit, loss[0, 0])


def solution(mesh):
    torus = Mesh(mesh.devices.reshape(4, 4, 2, 4), ("z", "y", "c", "x"))
    dp = ("z", "y", "c")
    in_specs = (
        P(dp, "x"), P(dp, "x"), P(dp, "x"), P(dp, "x"), P("x", dp), P("x"), P(dp, "x"), P(dp, "x"),
    )
    out_specs = (P(dp, "x"), P(dp, "x"), P(dp, "x"), P())
    return jax.shard_map(body, mesh=torus, in_specs=in_specs, out_specs=out_specs, check_vma=False)
```
